256 devices in a mesh: band: 8 (over z_hi, core), dom: 32 (over y, x, z_lo).
Axes of the slice: x: 4, y: 4, z: 8 (z_hi: 4, z_lo: 2; z = z_hi * 2 + z_lo), core: 2. Of those that a mesh axis runs over, the one named last changes fastest.
Arguments:
- orbital_block: bfloat16 [8192, 4096], P('dom', 'band'), may hold values from -6 to 6
- cell_matrices: bfloat16 [128, 125, 125], P('dom'), may hold values from -0.09 to 0.09, as said below
- cell_nodes: int32 [125, 128], P(None, 'dom'), may hold values from 0 to 319, as said below
- shared_nodes: int32 [32, 64], P('dom'), may hold values from 0 to 255, as said below
- inv_sqrt_mass: float32 [8192], P('dom'), may hold values from 0.8 to 1.25
- potential: float32 [8192], P('dom'), may hold values from -0.5 to 0.3
- filter_center: float32 [1], replicated, may hold values from -0.1 to 0.1
- filter_halfwidth: float32 [1], replicated, may hold values from 0.8 to 1.2
Outputs:
- filtered: bfloat16 [8192, 4096], P('dom', 'band')
- intersection: float32 [4096, 4096], P(('band', 'dom'))
- projected: float32 [4096, 4096], P(('band', 'dom'))
The draws below stay inside these ranges and needn't reach their ends.
Inputs may be any that keep to these rules, and one draw needn't show every extreme that they name: `cell_matrices`: each cell's matrix is symmetric. `cell_nodes`: column c lists the 125 nodes of cell c, a hexahedron of degree 4 with its nodes in lexicographic order, numbered as the device that holds the cell sees them: a value below 256 is one of its own nodes, a value 256 + j is entry j of the next device's (cyclically) shared list. Every own node and every shared entry is used by some cell. `shared_nodes`: row d holds 64 distinct own nodes of device d, which cells of device d - 1 (cyclically) also use.
All inputs are finite; a program needn't handle non-finite values.
Results may differ from the reference program's by a relative error of at most 0.024.
Values may be sent and summed in bfloat16 or wider, within the bound.
A program may use at most 64 MiB of HBM per device.

```python
import math
import jax
import jax.numpy as jnp
from jax import lax

ORB_BLK = 512
FILTER_DEG = 4
CY = 2
CZ = 2
CELLS_DEV = 4
PLANE = 64
NODES_DEV = 256
NODES_ALL = 8192
CELLS_ALL = 128
ORB = 4096
N_BAND = 8
N_DOM = 32


def mesh_tables(key):
    span_y = 4 * CY
    span_z = 4 * CZ
    perm_keys = jax.random.split(jax.random.fold_in(key, 4242), N_DOM)
    orders = jax.vmap(lambda one_key: jax.random.permutation(one_key, NODES_DEV))(perm_keys).astype(jnp.int32)
    corner = jnp.arange(125, dtype=jnp.int32)
    along_x = corner // 25
    along_y = corner // 5 % 5
    along_z = corner % 5
    cells = jnp.arange(CELLS_DEV, dtype=jnp.int32)
    cell_y = cells // CZ
    cell_z = cells % CZ
    ypos = (4 * cell_y[None, :] + along_y[:, None]) % span_y
    zpos = (4 * cell_z[None, :] + along_z[:, None]) % span_z
    xpos = jnp.broadcast_to(along_x[:, None], ypos.shape)
    inplane = ypos * span_z + zpos
    canon = jnp.minimum(xpos, 3) * span_y * span_z + inplane

    def per_device(order):
        return jnp.where(xpos < 4, order[canon], NODES_DEV + inplane).astype(jnp.int32)
    tables = jax.vmap(per_device)(orders)
    cell_table = jnp.transpose(tables, (1, 0, 2)).reshape(125, N_DOM * CELLS_DEV)
    shared = orders[:, :PLANE]
    return (cell_table.astype(jnp.int32), shared.astype(jnp.int32))


def draw_cell_nodes(key, part):
    return mesh_tables(key)[0]


def draw_shared_nodes(key, part):
    return mesh_tables(key)[1]


def draw_cell_matrices(key, part):
    spread = 4000.0 ** (-0.5)
    inner = jax.random.fold_in(key, 777)
    raw = jax.random.normal(inner, (CELLS_ALL, 125, 125), jnp.float32) * spread
    sym = (raw + jnp.transpose(raw, (0, 2, 1))) * 0.70710678
    return jnp.clip(sym, -0.09, 0.09).astype(jnp.bfloat16)


def block_levels(rng, extent, cuts, smallest, high):
    def one(position, shards_of):
        steps = jax.random.uniform(jax.random.fold_in(jax.random.fold_in(rng, 6), position), (shards_of,), jnp.float32, smallest / len(cuts), high / len(cuts))
        return jnp.repeat(jnp.exp(steps), extent[position] // shards_of).reshape((-1,) + (1,) * (len(extent) - position - 1))

    loudness = one(*cuts[0])
    for cut in cuts[1:]:
        loudness = loudness * one(*cut)
    return loudness


def noise(key, dims, deviation, most, shards=(), kind=jnp.bfloat16):
    array = jax.random.normal(key, dims, jnp.float32) * deviation
    if len(shards) > 0:
        array = block_levels(key, dims, shards, -0.22, 0.18) * array
    return jnp.clip(array, min=-most, max=most).astype(kind)


def setup_inputs(seed: int = 0) -> dict:
    streams_of = jax.random.split(jax.random.key(seed), 9)
    return {
        "orbital_block": noise(streams_of[0], (NODES_ALL, ORB), 1.0, 6.0, ((0, 32), (1, 8))),
        "cell_matrices": draw_cell_matrices(jax.random.fold_in(streams_of[8], 71), 0),
        "cell_nodes": draw_cell_nodes(jax.random.fold_in(streams_of[8], 71), 0),
        "shared_nodes": draw_shared_nodes(jax.random.fold_in(streams_of[8], 71), 0),
        "inv_sqrt_mass": jnp.clip(jnp.exp(math.log(1.25) - 0.4462871 * jax.random.uniform(streams_of[4], (NODES_ALL,), jnp.float32) ** block_levels(streams_of[4], (NODES_ALL,), ((0, 32),), -0.2, 0.2)), 0.8, 1.25),
        "potential": jnp.clip(-0.5 + 0.8 * jax.random.uniform(streams_of[5], (NODES_ALL,), jnp.float32) ** block_levels(streams_of[5], (NODES_ALL,), ((0, 32),), -0.2, 0.2), -0.5, 0.3),
        "filter_center": jnp.clip(jax.random.uniform(streams_of[6], (1,), jnp.float32, -0.1, 0.1), -0.1, 0.1),
        "filter_halfwidth": jnp.clip(jax.random.uniform(streams_of[7], (1,), jnp.float32, 0.8, 1.2), 0.8, 1.2),
    }


def hamilton(field, global_nodes, cell_matrices, inv_sqrt_mass, potential):
    scaled = (inv_sqrt_mass[:, None] * field).astype(jnp.bfloat16)
    gathered = scaled[global_nodes].astype(jnp.float32)
    cell_out = jnp.einsum('cij,jck->ick', cell_matrices.astype(jnp.float32), gathered)
    columns = field.shape[1]
    assembled = jnp.zeros(field.shape, jnp.float32).at[global_nodes.reshape(-1)].add(cell_out.reshape(-1, columns))
    return inv_sqrt_mass[:, None] * assembled + potential[:, None] * field

def reference(orbital_block, cell_matrices, cell_nodes, shared_nodes, inv_sqrt_mass, potential, filter_center, filter_halfwidth):
    cell_dev = jnp.arange(CELLS_ALL, dtype=jnp.int32) // CELLS_DEV
    next_dev = (cell_dev + 1) % N_DOM
    ghost_slot = jnp.clip(cell_nodes - NODES_DEV, 0, PLANE - 1).astype(jnp.int32)
    remote = next_dev[None, :] * NODES_DEV + shared_nodes[next_dev[None, :], ghost_slot]
    global_nodes = jnp.where(cell_nodes < NODES_DEV, cell_dev[None, :] * NODES_DEV + cell_nodes, remote).astype(jnp.int32)

    def mapped(field):
        applied_field = hamilton(field, global_nodes, cell_matrices, inv_sqrt_mass, potential)
        return (applied_field - filter_center[0] * field) / filter_halfwidth[0]

    def filter_one(columns):
        previous = columns.astype(jnp.float32)
        current = mapped(previous)
        for degree_step in range(FILTER_DEG - 1):
            following = 2.0 * mapped(current) - previous
            previous = current
            current = following
        filtered_part = current.astype(jnp.bfloat16)
        applied_part = hamilton(filtered_part.astype(jnp.float32), global_nodes, cell_matrices, inv_sqrt_mass, potential).astype(jnp.bfloat16)
        return (filtered_part, applied_part)
    pieces = orbital_block.reshape(NODES_ALL, N_BAND, ORB_BLK).transpose(1, 0, 2)
    filtered_blocks, applied_blocks = lax.map(filter_one, pieces)
    filtered = filtered_blocks.transpose(1, 0, 2).reshape(NODES_ALL, ORB)
    applied = applied_blocks.transpose(1, 0, 2).reshape(NODES_ALL, ORB)
    factor = 1.0 / NODES_ALL
    intersection = jnp.dot(filtered.T, filtered, preferred_element_type=jnp.float32) * factor
    projected = jnp.dot(filtered.T, applied, preferred_element_type=jnp.float32) * factor
    return (filtered, intersection, projected)
```

```python
import jax
import jax.numpy as jnp
from jax import lax
from jax.experimental import pallas as pl
from jax.experimental.pallas import tpu as pltpu
from jax.sharding import PartitionSpec as P

FILTER_DEG = 4
BF = jnp.bfloat16
F32 = jnp.float32
MESH = pl.DeviceIdType.MESH
ORDER = (0, 7, 1, 6, 2, 5, 3, 4)


def nn(a, b):
    return lax.dot_general(a, b, (((1,), (0,)), ((), ())), preferred_element_type=F32)


def nt(a, b):
    return lax.dot_general(a, b, (((1,), (1,)), ((), ())), preferred_element_type=F32)


def split(a):
    hi = a.astype(BF)
    return hi, (a - hi.astype(F32)).astype(BF)


def rows_equal(count, row, base=0):
    index = lax.broadcasted_iota(jnp.int32, (count, row.shape[1]), 0) + base
    return jnp.where(index == row, 1.0, 0.0).astype(BF)


def kernel(
    x_ref, m_ref, ints_ref, vecs_ref, scal_ref,
    filt_ref, inter_ref, proj_ref,
    xp, xc, m2, ints2, vecs2, perm,
    gt0, u0, gt1, u1, kmat, k1, ahi, alo, w2, w2t, kgg_out, kgg_in,
    invb, invl, potb, potl, vcur, vprev, sbuf, gc_out, gc_in,
    fall, fat, p1, r1a, r1b, p2, r2a, r2b, sfin, fin,
    loc_sem, set_s, set_r, kgg_s, kgg_r, halo_s, halo_r,
    zs, zr, cs, cr, rs_s, rs_r,
):
    band = lax.axis_index("band")
    dom = lax.axis_index("dom")
    zh, core = band // 2, band % 2
    zl, x, y = dom % 2, (dom // 2) % 4, dom // 8
    z = zh * 2 + zl

    def device(zz, yy, xx, cc):
        return ((zz // 2) * 2 + cc, (yy * 4 + xx) * 2 + zz % 2)

    z_up, z_down = device((z + 1) % 8, y, x, core), device((z + 7) % 8, y, x, core)
    x_up, x_down = device(z, y, (x + 1) % 4, core), device(z, y, (x + 3) % 4, core)
    y_up, y_down = device(z, (y + 1) % 4, x, core), device(z, (y + 3) % 4, x, core)
    mate = device(z, y, x, 1 - core)
    pair = device(zh * 2 + 1 - zl, y, x, core)
    slab = y * 4 + x
    after, before = (slab + 1) % 16, (slab + 15) % 16
    nxt = device(z, after // 4, after % 4, core)
    prv = device(z, before // 4, before % 4, core)

    barrier = pltpu.get_barrier_semaphore()
    friends = (z_up, z_down, x_up, x_down, y_up, y_down, mate, nxt, prv)
    for friend in friends:
        pl.semaphore_signal(barrier, inc=1, device_id=friend, device_id_type=MESH)

    def send(src, dst, ssem, rsem, to):
        copy = pltpu.make_async_remote_copy(
            src_ref=src, dst_ref=dst, send_sem=ssem, recv_sem=rsem,
            device_id=to, device_id_type=MESH,
        )
        copy.start()
        return copy

    started = []

    col = lax.broadcasted_iota(jnp.int32, (512, 512), 0)
    place = lax.broadcasted_iota(jnp.int32, (512, 512), 1)
    goal = ((col >> 4) & 1) * 256 + (col >> 5) * 16 + (col & 15)
    perm[...] = jnp.where(goal == place, 1.0, 0.0).astype(BF)
    for half in range(2):
        xp[half] = nn(x_ref[...], perm[:, half * 256 : half * 256 + 256]).astype(BF)

    pl.semaphore_wait(barrier, len(friends))
    setup = [
        send(m_ref, m2.at[zl], set_s.at[0], set_r.at[0], pair),
        send(ints_ref, ints2.at[zl], set_s.at[1], set_r.at[1], pair),
        send(vecs_ref, vecs2.at[zl], set_s.at[2], set_r.at[2], pair),
        send(xp.at[1 - zl], xc.at[zl], set_s.at[3], set_r.at[3], pair),
    ]
    started += setup
    own = [
        pltpu.make_async_copy(m_ref, m2.at[zl], loc_sem.at[0]),
        pltpu.make_async_copy(ints_ref, ints2.at[zl], loc_sem.at[1]),
        pltpu.make_async_copy(vecs_ref, vecs2.at[zl], loc_sem.at[2]),
        pltpu.make_async_copy(xp.at[zl], xc.at[zl], loc_sem.at[3]),
    ]
    for copy in own:
        copy.start()
    for copy in own:
        copy.wait()
    kgg_in[64:128] = jnp.zeros((64, 128), F32)
    for copy in setup:
        copy.wait_recv()

    q1t = rows_equal(256, ints2[1, 4:5, :])
    q0t = rows_equal(256, ints2[0, 4:5, :])
    q0t_right = rows_equal(256, ints2[0, 5:6, :])
    for c in range(4):
        lanes = slice(c * 128, c * 128 + 128)
        row = ints2[0, c : c + 1, :]
        top = rows_equal(256, row)
        ghost = rows_equal(128, row, 256)
        bottom = nn(q1t, ghost).astype(BF)
        gt0[0:256, lanes] = top
        gt0[256:512, lanes] = bottom
        u0[0:256, lanes] = nn(top, m2[0, c]).astype(BF)
        u0[256:512, lanes] = nn(bottom, m2[0, c]).astype(BF)
        hot = rows_equal(384, ints2[1, c : c + 1, :])
        gt1[:, lanes] = hot
        u1[:, lanes] = nn(hot, m2[1, c]).astype(BF)
    k1[...] = nt(u1[...], gt1[...])
    kmat[...] = nt(u0[...], gt0[...])
    kmat[256:512, 256:512] += k1[0:256, 0:256]
    kgg_out[...] = k1[256:320, 256:384]
    kgg = send(kgg_out, kgg_in.at[0:64], kgg_s, kgg_r, nxt)
    started.append(kgg)
    w2[0, 0:256] = q0t_right
    w2[1, 0:256] = jnp.zeros((256, 128), BF)
    hi, lo = split(k1[0:256, 256:384])
    w2[0, 256:512] = hi
    w2[1, 256:512] = lo
    eye = jnp.where(
        lax.broadcasted_iota(jnp.int32, (128, 128), 0)
        == lax.broadcasted_iota(jnp.int32, (128, 128), 1),
        1.0,
        0.0,
    ).astype(BF)
    w2t[0, :, 0:256] = nt(eye, q0t_right).astype(BF)
    w2t[1, :, 0:256] = jnp.zeros((128, 256), BF)
    hi, lo = split(k1[256:384, 0:256])
    w2t[0, :, 256:512] = hi
    w2t[1, :, 256:512] = lo

    center, halfwidth = scal_ref[0], scal_ref[1]
    for slot in range(2):
        nodes = slice(slot * 256, slot * 256 + 256)
        columns = jnp.transpose(vecs2[slot])
        mass = jnp.broadcast_to(columns[:, 0:1], (256, 256))
        pot = jnp.broadcast_to(columns[:, 1:2], (256, 256))
        invb[nodes] = mass
        potb[nodes] = pot
        invl[nodes] = mass / halfwidth
        potl[nodes] = (pot - center) / halfwidth
        start = xc[slot].astype(F32)
        vcur[nodes] = start
        sbuf[nodes] = (mass * start).astype(BF)

    def exchange(step):
        out = nn(w2t[0], sbuf[...]) + nn(w2t[1], sbuf[...])
        gc_out[step] = out.astype(BF)
        forth = send(
            gc_out.at[step, 0:64], gc_in.at[step, 64:128],
            halo_s.at[step, 0], halo_r.at[step, 0], nxt,
        )
        back = send(
            gc_out.at[step, 64:128], gc_in.at[step, 0:64],
            halo_s.at[step, 1], halo_r.at[step, 1], prv,
        )
        started.extend([forth, back])
        return forth, back

    def assemble(step, copies):
        inner = nn(ahi[...], sbuf[...]) + nn(alo[...], sbuf[...])
        for copy in copies:
            copy.wait_recv()
        came = gc_in[step]
        return inner + nn(w2[0], came) + nn(w2[1], came)

    copies = exchange(0)
    kgg.wait_recv()
    hi, lo = split(kgg_in[...])
    hi, lo = split(nn(q0t, hi) + nn(q0t, lo))
    kmat[0:256, 0:256] += nt(hi, q0t) + nt(lo, q0t)
    hi, lo = split(kmat[...])
    ahi[...] = hi
    alo[...] = lo

    for step in range(FILTER_DEG):
        if step > 0:
            copies = exchange(step)
        total = assemble(step, copies)
        image = invl[...] * total + potl[...] * vcur[...]
        if step > 0:
            image = 2.0 * image - vprev[...]
        if step < FILTER_DEG - 1:
            vprev[...] = vcur[...]
            vcur[...] = image
            sbuf[...] = (invb[...] * image).astype(BF)
        else:
            filtered = image.astype(BF)
            fall[0, core] = filtered
            wide = filtered.astype(F32)
            vcur[...] = wide
            sbuf[...] = (invb[...] * wide).astype(BF)

    def up(slot, k):
        src, dst = fall.at[slot, core], fall.at[(slot + 7) % 8, core]
        if k == 3:
            src, dst = src.at[0:256], dst.at[0:256]
        started.append(send(src, dst, zs.at[0, k], zr.at[0, k], z_up))
        return started[-1]

    def down(slot, k):
        src, dst = fall.at[slot, core], fall.at[(slot + 1) % 8, core]
        if k == 3:
            src, dst = src.at[256:512], dst.at[256:512]
        started.append(send(src, dst, zs.at[1, k], zr.at[1, k], z_down))
        return started[-1]

    def across(slot):
        block = fall.at[slot, core]
        started.append(send(block, block, cs.at[slot], cr.at[slot], mate))
        return started[-1]

    ups, downs, others = [up(0, 0)], [down(0, 0)], {0: across(0)}

    copies = exchange(FILTER_DEG)
    total = assemble(FILTER_DEG, copies)
    applied = invb[...] * total + potb[...] * vcur[...]
    fat[0:256] = jnp.transpose(vcur[...]).astype(BF)
    vprev[...] = applied
    fat[256:512] = jnp.transpose(vprev[...]).astype(BF)

    def arrive(slot):
        if slot >= 5:
            k = 7 - slot
            ups[k].wait_recv()
            ups.append(up(slot, k + 1))
            others[slot] = across(slot)
        elif 1 <= slot <= 3:
            k = slot - 1
            downs[k].wait_recv()
            downs.append(down(slot, k + 1))
            others[slot] = across(slot)
        elif slot == 4:
            ups[3].wait_recv()
            downs[3].wait_recv()
            others[slot] = across(slot)

    lines = (((x, x_up, x_down), (y, y_up, y_down)), ((y, y_up, y_down), (x, x_up, x_down)))
    flights = {}

    def ring_first(piece, mat, level):
        pos, right, left = lines[mat][level]
        part, in_a = (p1, r1a) if level == 0 else (p2, r2a)
        far = (pos + 2) % 4
        sem = (piece, mat, level)
        pairs = []
        for side, to in ((0, right), (1, left)):
            pairs.append(send(
                part.at[piece, mat, far, side], in_a.at[piece, mat, side],
                rs_s.at[(*sem, side)], rs_r.at[(*sem, side)], to,
            ))
        flights[(*sem, 0)] = pairs
        started.extend(pairs)

    def ring_second(piece, mat, level):
        pos, right, left = lines[mat][level]
        part, in_a, in_b = (p1, r1a, r1b) if level == 0 else (p2, r2a, r2b)
        sem = (piece, mat, level)
        pairs = []
        for side, to in ((0, right), (1, left)):
            near = (pos + 1) % 4 if side == 0 else (pos + 3) % 4
            flights[(*sem, 0)][side].wait_recv()
            whole = part[piece, mat, near, side].astype(F32) + in_a[piece, mat, side].astype(F32)
            part[piece, mat, near, side] = whole.astype(BF)
            pairs.append(send(
                part.at[piece, mat, near], in_b.at[piece, mat, side],
                rs_s.at[(*sem, 2 + side)], rs_r.at[(*sem, 2 + side)], to,
            ))
        flights[(*sem, 1)] = pairs
        started.extend(pairs)

    def ring_last(piece, mat, level):
        pos, right, left = lines[mat][level]
        part, in_b = (p1, r1b) if level == 0 else (p2, r2b)
        for copy in flights[(piece, mat, level, 1)]:
            copy.wait_recv()
        return (
            part[piece, mat, pos].astype(F32)
            + in_b[piece, mat, 0].astype(F32)
            + in_b[piece, mat, 1].astype(F32)
        )

    def stage(number, piece):
        slot = ORDER[piece]
        if number == 0:
            arrive(slot)
            others[slot].wait_recv()
            for side in range(2):
                product = nn(fat[...], fall[slot, side]).astype(BF)
                for yy in range(4):
                    for xx in range(4):
                        k = (yy * 4 + xx) * 16
                        p1[piece, 0, xx, side, yy * 16 : yy * 16 + 16] = product[k : k + 16]
                    k = 256 + yy * 64
                    p1[piece, 1, yy, side] = product[k : k + 64]
            for mat in range(2):
                ring_first(piece, mat, 0)
        elif number == 1:
            for mat in range(2):
                ring_second(piece, mat, 0)
        elif number == 2:
            for mat in range(2):
                level_sum = ring_last(piece, mat, 0).astype(BF)
                for to in range(4):
                    p2[piece, mat, to] = level_sum[:, to * 16 : to * 16 + 16]
                ring_first(piece, mat, 1)
        elif number == 3:
            for mat in range(2):
                ring_second(piece, mat, 1)
        else:
            source = (z + slot) % 8
            for mat in range(2):
                sfin[source, :, mat] = ring_last(piece, mat, 1)

    for tick in range(12):
        for number in range(4, -1, -1):
            piece = tick - number
            if 0 <= piece < 8:
                stage(number, piece)

    mine = pl.ds(pl.multiple_of(zl * 256, 256), 256)
    filt_ref[...] = (
        nt(fall[zl * 7, core, mine], perm[:, 0:256]) + nt(fall[1 - zl, core, mine], perm[:, 256:512])
    ).astype(BF)
    factor = 1.0 / 8192
    for group in range(8):
        lines_of = slice(group * 32, group * 32 + 32)
        for half in range(2):
            block = sfin[(group // 2) * 2 + half, group % 2].reshape(32, 256)
            hi, lo = split(block)
            fin[0, lines_of, half * 256 : half * 256 + 256] = hi
            fin[1, lines_of, half * 256 : half * 256 + 256] = lo
    result = (nt(fin[0], perm[...]) + nt(fin[1], perm[...])) * factor
    for group in range(8):
        lanes = slice(group * 512, group * 512 + 512)
        inter_ref[:, lanes] = result[group * 32 : group * 32 + 16]
        proj_ref[:, lanes] = result[group * 32 + 16 : group * 32 + 32]
    for copy in started:
        copy.wait_send()


def shards(
    orbital_block,
    cell_matrices,
    cell_nodes,
    shared_nodes,
    inv_sqrt_mass,
    potential,
    filter_center,
    filter_halfwidth,
):
    matrices = jnp.pad(cell_matrices, ((0, 0), (0, 3), (0, 3)))
    nodes = jnp.pad(cell_nodes.T, ((0, 0), (0, 3)), constant_values=-1)
    shared = jnp.concatenate(
        [
            jnp.pad(shared_nodes, ((0, 0), (0, 64)), constant_values=-1),
            jnp.pad(shared_nodes, ((0, 0), (64, 0)), constant_values=-1),
        ]
    )
    ints = jnp.pad(jnp.concatenate([nodes, shared]), ((0, 2), (0, 0)), constant_values=-1)
    vecs = jnp.pad(jnp.stack([inv_sqrt_mass, potential]), ((0, 6), (0, 0)))
    scal = jnp.concatenate([filter_center, filter_halfwidth])
    vm = pl.BlockSpec(memory_space=pltpu.VMEM)
    V = pltpu.VMEM
    dma = pltpu.SemaphoreType.DMA
    return pl.pallas_call(
        kernel,
        out_shape=(
            jax.ShapeDtypeStruct((256, 512), BF),
            jax.ShapeDtypeStruct((16, 4096), F32),
            jax.ShapeDtypeStruct((16, 4096), F32),
        ),
        in_specs=[vm, vm, vm, vm, pl.BlockSpec(memory_space=pltpu.SMEM)],
        out_specs=(vm, vm, vm),
        scratch_shapes=[
            V((2, 256, 256), BF),
            V((2, 256, 256), BF),
            V((2, 4, 128, 128), BF),
            V((2, 8, 128), jnp.int32),
            V((2, 8, 256), F32),
            V((512, 512), BF),
            V((512, 512), BF),
            V((512, 512), BF),
            V((384, 512), BF),
            V((384, 512), BF),
            V((512, 512), F32),
            V((384, 384), F32),
            V((512, 512), BF),
            V((512, 512), BF),
            V((2, 512, 128), BF),
            V((2, 128, 512), BF),
            V((64, 128), F32),
            V((128, 128), F32),
            V((512, 256), F32),
            V((512, 256), F32),
            V((512, 256), F32),
            V((512, 256), F32),
            V((512, 256), F32),
            V((512, 256), F32),
            V((512, 256), BF),
            V((FILTER_DEG + 1, 128, 256), BF),
            V((FILTER_DEG + 1, 128, 256), BF),
            V((8, 2, 512, 256), BF),
            V((512, 512), BF),
            V((8, 2, 4, 2, 64, 256), BF),
            V((8, 2, 2, 64, 256), BF),
            V((8, 2, 2, 2, 64, 256), BF),
            V((8, 2, 4, 2, 16, 256), BF),
            V((8, 2, 2, 16, 256), BF),
            V((8, 2, 2, 2, 16, 256), BF),
            V((8, 2, 2, 16, 256), F32),
            V((2, 256, 512), BF),
            dma((4,)),
            dma((4,)),
            dma((4,)),
            dma,
            dma,
            dma((FILTER_DEG + 1, 2)),
            dma((FILTER_DEG + 1, 2)),
            dma((2, 4)),
            dma((2, 4)),
            dma((8,)),
            dma((8,)),
            dma((8, 2, 2, 4)),
            dma((8, 2, 2, 4)),
        ],
        compiler_params=pltpu.CompilerParams(
            collective_id=0, has_side_effects=True, vmem_limit_bytes=56 * 1024 * 1024
        ),
    )(orbital_block, matrices, ints, vecs, scal)


def solution(mesh):
    return jax.shard_map(
        shards,
        mesh=mesh,
        in_specs=(
            P("dom", "band"),
            P("dom", None, None),
            P(None, "dom"),
            P("dom", None),
            P("dom"),
            P("dom"),
            P(),
            P(),
        ),
        out_specs=(P("dom", "band"), P(("band", "dom"), None), P(("band", "dom"), None)),
        check_vma=False,
    )
```

```python
import jax
import jax.numpy as jnp
from jax import lax
from jax.experimental import pallas as pl
from jax.experimental.pallas import tpu as pltpu
from jax.sharding import PartitionSpec as P

FILTER_DEG = 4
BF = jnp.bfloat16
F32 = jnp.float32
MESH = pl.DeviceIdType.MESH
ORDER = (0, 7, 1, 6, 2, 5, 3, 4)


def nn(a, b):
    return lax.dot_general(a, b, (((1,), (0,)), ((), ())), preferred_element_type=F32)


def nt(a, b):
    return lax.dot_general(a, b, (((1,), (1,)), ((), ())), preferred_element_type=F32)


def split(a):
    hi = a.astype(BF)
    return hi, (a - hi.astype(F32)).astype(BF)


def rows_equal(count, row, base=0):
    index = lax.broadcasted_iota(jnp.int32, (count, row.shape[1]), 0) + base
    return jnp.where(index == row, 1.0, 0.0).astype(BF)


def kernel(
    x_ref, m_ref, nodes_ref, shared_ref, mass_ref, pot_ref, center_ref, half_ref,
    filt_ref, inter_ref, proj_ref,
    mown, ints_own, vecs_own, xp, xc, m2, ints2, vecs2, perm,
    gt0, u0, gt1, u1, kmat, k1, ahi, alo, w2, w2t, kgg_out, kgg_in,
    invb, invl, potb, potl, vcur, vprev, sbuf, gc_out, gc_in,
    fall, fat, p1, r1a, r1b, p2, r2a, r2b, sfin, fin,
    loc_sem, set_s, set_r, kgg_s, kgg_r, halo_s, halo_r,
    zs, zr, cs, cr, rs_s, rs_r,
):
    band = lax.axis_index("band")
    dom = lax.axis_index("dom")
    zh, core = band // 2, band % 2
    zl, x, y = dom % 2, (dom // 2) % 4, dom // 8
    z = zh * 2 + zl

    def device(zz, yy, xx, cc):
        return ((zz // 2) * 2 + cc, (yy * 4 + xx) * 2 + zz % 2)

    z_up, z_down = device((z + 1) % 8, y, x, core), device((z + 7) % 8, y, x, core)
    x_up, x_down = device(z, y, (x + 1) % 4, core), device(z, y, (x + 3) % 4, core)
    y_up, y_down = device(z, (y + 1) % 4, x, core), device(z, (y + 3) % 4, x, core)
    mate = device(z, y, x, 1 - core)
    pair = device(zh * 2 + 1 - zl, y, x, core)
    slab = y * 4 + x
    after, before = (slab + 1) % 16, (slab + 15) % 16
    nxt = device(z, after // 4, after % 4, core)
    prv = device(z, before // 4, before % 4, core)

    barrier = pltpu.get_barrier_semaphore()
    friends = (z_up, z_down, x_up, x_down, y_up, y_down, mate, nxt, prv)
    for friend in friends:
        pl.semaphore_signal(barrier, inc=1, device_id=friend, device_id_type=MESH)

    def send(src, dst, ssem, rsem, to):
        copy = pltpu.make_async_remote_copy(
            src_ref=src, dst_ref=dst, send_sem=ssem, recv_sem=rsem,
            device_id=to, device_id_type=MESH,
        )
        copy.start()
        return copy

    started = []

    ints_own[...] = jnp.full((8, 128), -1, jnp.int32)
    ints_own[0:4, 0:125] = nodes_ref[...]
    ints_own[4:5, 0:64] = shared_ref[...]
    ints_own[5:6, 64:128] = shared_ref[...]
    vecs_own[...] = jnp.zeros_like(vecs_own)
    vecs_own[0:1] = mass_ref[...]
    vecs_own[1:2] = pot_ref[...]
    mown[...] = jnp.zeros_like(mown)
    mown[:, 0:125, 0:125] = m_ref[...]
    kgg_in[64:128] = jnp.zeros((64, 128), F32)

    pl.semaphore_wait(barrier, len(friends))
    setup = [
        send(ints_own, ints2.at[zl], set_s.at[0], set_r.at[0], pair),
        send(vecs_own, vecs2.at[zl], set_s.at[1], set_r.at[1], pair),
        send(mown, m2.at[zl], set_s.at[2], set_r.at[2], pair),
    ]
    own = [
        pltpu.make_async_copy(ints_own, ints2.at[zl], loc_sem.at[0]),
        pltpu.make_async_copy(vecs_own, vecs2.at[zl], loc_sem.at[1]),
        pltpu.make_async_copy(mown, m2.at[zl], loc_sem.at[2]),
    ]
    for copy in own:
        copy.start()
    col = lax.broadcasted_iota(jnp.int32, (512, 512), 0)
    place = lax.broadcasted_iota(jnp.int32, (512, 512), 1)
    goal = ((col >> 4) & 1) * 256 + (col >> 5) * 16 + (col & 15)
    perm[...] = jnp.where(goal == place, 1.0, 0.0).astype(BF)
    for half in range(2):
        xp[half] = nn(x_ref[...], perm[:, half * 256 : half * 256 + 256]).astype(BF)
    setup.append(send(xp.at[1 - zl], xc.at[zl], set_s.at[3], set_r.at[3], pair))
    own.append(pltpu.make_async_copy(xp.at[zl], xc.at[zl], loc_sem.at[3]))
    own[3].start()
    started += setup
    for copy in own[0:2]:
        copy.wait()
    for copy in setup[0:2]:
        copy.wait_recv()

    q1t = rows_equal(256, ints2[1, 4:5, :])
    q0t = rows_equal(256, ints2[0, 4:5, :])
    q0t_right = rows_equal(256, ints2[0, 5:6, :])
    for c in range(4):
        lanes = slice(c * 128, c * 128 + 128)
        row = ints2[0, c : c + 1, :]
        top = rows_equal(256, row)
        ghost = rows_equal(128, row, 256)
        bottom = nn(q1t, ghost).astype(BF)
        gt0[0:256, lanes] = top
        gt0[256:512, lanes] = bottom
        gt1[:, lanes] = rows_equal(384, ints2[1, c : c + 1, :])
    own[2].wait()
    setup[2].wait_recv()
    for c in range(4):
        lanes = slice(c * 128, c * 128 + 128)
        u1[:, lanes] = nn(gt1[:, lanes], m2[1, c]).astype(BF)
    for c in range(4):
        lanes = slice(c * 128, c * 128 + 128)
        u0[:, lanes] = nn(gt0[:, lanes], m2[0, c]).astype(BF)
    k1[...] = nt(u1[...], gt1[...])
    kgg_out[...] = k1[256:320, 256:384]
    kgg = send(kgg_out, kgg_in.at[0:64], kgg_s, kgg_r, nxt)
    started.append(kgg)
    kmat[...] = nt(u0[...], gt0[...])
    kmat[256:512, 256:512] += k1[0:256, 0:256]
    w2[0, 0:256] = q0t_right
    w2[1, 0:256] = jnp.zeros((256, 128), BF)
    hi, lo = split(k1[0:256, 256:384])
    w2[0, 256:512] = hi
    w2[1, 256:512] = lo
    eye = jnp.where(
        lax.broadcasted_iota(jnp.int32, (128, 128), 0)
        == lax.broadcasted_iota(jnp.int32, (128, 128), 1),
        1.0,
        0.0,
    ).astype(BF)
    w2t[0, :, 0:256] = nt(eye, q0t_right).astype(BF)
    w2t[1, :, 0:256] = jnp.zeros((128, 256), BF)
    hi, lo = split(k1[256:384, 0:256])
    w2t[0, :, 256:512] = hi
    w2t[1, :, 256:512] = lo

    center, halfwidth = center_ref[0], half_ref[0]
    own[3].wait()
    setup[3].wait_recv()
    for slot in range(2):
        nodes = slice(slot * 256, slot * 256 + 256)
        columns = jnp.transpose(vecs2[slot])
        mass = jnp.broadcast_to(columns[:, 0:1], (256, 256))
        pot = jnp.broadcast_to(columns[:, 1:2], (256, 256))
        invb[nodes] = mass
        potb[nodes] = pot
        invl[nodes] = mass / halfwidth
        potl[nodes] = (pot - center) / halfwidth
        start = xc[slot].astype(F32)
        vcur[nodes] = start
        sbuf[nodes] = (mass * start).astype(BF)

    def exchange(step):
        out = nn(w2t[0], sbuf[...]) + nn(w2t[1], sbuf[...])
        gc_out[step] = out.astype(BF)
        forth = send(
            gc_out.at[step, 0:64], gc_in.at[step, 64:128],
            halo_s.at[step, 0], halo_r.at[step, 0], nxt,
        )
        back = send(
            gc_out.at[step, 64:128], gc_in.at[step, 0:64],
            halo_s.at[step, 1], halo_r.at[step, 1], prv,
        )
        started.extend([forth, back])
        return forth, back

    def assemble(step, copies):
        inner = nn(ahi[...], sbuf[...]) + nn(alo[...], sbuf[...])
        for copy in copies:
            copy.wait_recv()
        came = gc_in[step]
        return inner + nn(w2[0], came) + nn(w2[1], came)

    copies = exchange(0)
    kgg.wait_recv()
    hi, lo = split(kgg_in[...])
    hi, lo = split(nn(q0t, hi) + nn(q0t, lo))
    kmat[0:256, 0:256] += nt(hi, q0t) + nt(lo, q0t)
    hi, lo = split(kmat[...])
    ahi[...] = hi
    alo[...] = lo

    for step in range(FILTER_DEG):
        if step > 0:
            copies = exchange(step)
        total = assemble(step, copies)
        image = invl[...] * total + potl[...] * vcur[...]
        if step > 0:
            image = 2.0 * image - vprev[...]
        if step < FILTER_DEG - 1:
            vprev[...] = vcur[...]
            vcur[...] = image
            sbuf[...] = (invb[...] * image).astype(BF)
        else:
            filtered = image.astype(BF)
            fall[0, core] = filtered
            wide = filtered.astype(F32)
            vcur[...] = wide
            sbuf[...] = (invb[...] * wide).astype(BF)

    tours = ([], [])

    def onward(way, slot, half):
        landing = (slot + 7) % 8 if way == 0 else (slot + 1) % 8
        nodes = slice(half * 256, half * 256 + 256)
        number = len(tours[way])
        copy = send(
            fall.at[slot, core, nodes], fall.at[landing, core, nodes],
            zs.at[way, number], zr.at[way, number], (z_up, z_down)[way],
        )
        tours[way].append((copy, landing, half))
        started.append(copy)

    others = {}

    def across(slot, half):
        block = fall.at[slot, core, half * 256 : half * 256 + 256]
        others[slot, half] = send(block, block, cs.at[slot, half], cr.at[slot, half], mate)
        started.append(others[slot, half])

    def arrive(number):
        for way in range(2):
            copy, slot, half = tours[way][number]
            copy.wait_recv()
            if number < 5:
                onward(way, slot, half)
            across(slot, half)

    for half in range(2):
        onward(0, 0, half)
        onward(1, 0, 1 - half)
    for half in range(2):
        across(0, half)

    copies = exchange(FILTER_DEG)
    total = assemble(FILTER_DEG, copies)
    applied = invb[...] * total + potb[...] * vcur[...]
    arrive(0)
    fat[0:256] = jnp.transpose(vcur[...]).astype(BF)
    vprev[...] = applied
    fat[256:512] = jnp.transpose(vprev[...]).astype(BF)

    lines = (((x, x_up, x_down), (y, y_up, y_down)), ((y, y_up, y_down), (x, x_up, x_down)))
    flights = {}

    def ring_first(piece, mat, level):
        pos, right, left = lines[mat][level]
        part, in_a = (p1, r1a) if level == 0 else (p2, r2a)
        far = (pos + 2) % 4
        sem = (piece, mat, level)
        pairs = []
        for side, to in ((0, right), (1, left)):
            pairs.append(send(
                part.at[piece, mat, far, side], in_a.at[piece, mat, side],
                rs_s.at[(*sem, side)], rs_r.at[(*sem, side)], to,
            ))
        flights[(*sem, 0)] = pairs
        started.extend(pairs)

    def ring_second(piece, mat, level):
        pos, right, left = lines[mat][level]
        part, in_a, in_b = (p1, r1a, r1b) if level == 0 else (p2, r2a, r2b)
        sem = (piece, mat, level)
        pairs = []
        for side, to in ((0, right), (1, left)):
            near = (pos + 1) % 4 if side == 0 else (pos + 3) % 4
            flights[(*sem, 0)][side].wait_recv()
            whole = part[piece, mat, near, side].astype(F32) + in_a[piece, mat, side].astype(F32)
            part[piece, mat, near, side] = whole.astype(BF)
            pairs.append(send(
                part.at[piece, mat, near], in_b.at[piece, mat, side],
                rs_s.at[(*sem, 2 + side)], rs_r.at[(*sem, 2 + side)], to,
            ))
        flights[(*sem, 1)] = pairs
        started.extend(pairs)

    def ring_last(piece, mat, level):
        pos, right, left = lines[mat][level]
        part, in_b = (p1, r1b) if level == 0 else (p2, r2b)
        for copy in flights[(piece, mat, level, 1)]:
            copy.wait_recv()
        return (
            part[piece, mat, pos].astype(F32)
            + in_b[piece, mat, 0].astype(F32)
            + in_b[piece, mat, 1].astype(F32)
        )

    def stage(number, piece):
        slot = ORDER[piece]
        if number == 0:
            for turn in range(2):
                side = core if turn == 0 else 1 - core
                if turn == 1:
                    for half in range(2):
                        others[slot, half].wait_recv()
                product = nn(fat[...], fall[slot, side]).astype(BF)
                for yy in range(4):
                    for xx in range(4):
                        k = (yy * 4 + xx) * 16
                        p1[piece, 0, xx, side, yy * 16 : yy * 16 + 16] = product[k : k + 16]
                    k = 256 + yy * 64
                    p1[piece, 1, yy, side] = product[k : k + 64]
            for mat in range(2):
                ring_first(piece, mat, 0)
        elif number == 1:
            for mat in range(2):
                ring_second(piece, mat, 0)
        elif number == 2:
            for mat in range(2):
                level_sum = ring_last(piece, mat, 0).astype(BF)
                for to in range(4):
                    p2[piece, mat, to] = level_sum[:, to * 16 : to * 16 + 16]
                ring_first(piece, mat, 1)
        elif number == 3:
            for mat in range(2):
                ring_second(piece, mat, 1)
        else:
            source = (z + slot) % 8
            for mat in range(2):
                sfin[source, :, mat] = ring_last(piece, mat, 1)

    for tick in range(16):
        if 1 <= tick <= 6:
            arrive(tick)
        for number in range(4, -1, -1):
            piece = tick - 2 * number
            if 0 <= piece < 8:
                stage(number, piece)
        if tick == 8:
            mine = pl.ds(pl.multiple_of(zl * 256, 256), 256)
            filt_ref[...] = (
                nt(fall[zl * 7, core, mine], perm[:, 0:256])
                + nt(fall[1 - zl, core, mine], perm[:, 256:512])
            ).astype(BF)

    factor = 1.0 / 8192
    for group in range(8):
        lines_of = slice(group * 32, group * 32 + 32)
        for half in range(2):
            block = sfin[(group // 2) * 2 + half, group % 2].reshape(32, 256)
            hi, lo = split(block)
            fin[0, lines_of, half * 256 : half * 256 + 256] = hi
            fin[1, lines_of, half * 256 : half * 256 + 256] = lo
    result = (nt(fin[0], perm[...]) + nt(fin[1], perm[...])) * factor
    for group in range(8):
        lanes = slice(group * 512, group * 512 + 512)
        inter_ref[:, lanes] = result[group * 32 : group * 32 + 16]
        proj_ref[:, lanes] = result[group * 32 + 16 : group * 32 + 32]
    for copy in started:
        copy.wait_send()


def shards(
    orbital_block,
    cell_matrices,
    cell_nodes,
    shared_nodes,
    inv_sqrt_mass,
    potential,
    filter_center,
    filter_halfwidth,
):
    vm = pl.BlockSpec(memory_space=pltpu.VMEM)
    sm = pl.BlockSpec(memory_space=pltpu.SMEM)
    V = pltpu.VMEM
    dma = pltpu.SemaphoreType.DMA
    return pl.pallas_call(
        kernel,
        out_shape=(
            jax.ShapeDtypeStruct((256, 512), BF),
            jax.ShapeDtypeStruct((16, 4096), F32),
            jax.ShapeDtypeStruct((16, 4096), F32),
        ),
        in_specs=[vm, vm, vm, vm, vm, vm, sm, sm],
        out_specs=(vm, vm, vm),
        scratch_shapes=[
            V((4, 128, 128), BF),
            V((8, 128), jnp.int32),
            V((8, 256), F32),
            V((2, 256, 256), BF),
            V((2, 256, 256), BF),
            V((2, 4, 128, 128), BF),
            V((2, 8, 128), jnp.int32),
            V((2, 8, 256), F32),
            V((512, 512), BF),
            V((512, 512), BF),
            V((512, 512), BF),
            V((384, 512), BF),
            V((384, 512), BF),
            V((512, 512), F32),
            V((384, 384), F32),
            V((512, 512), BF),
            V((512, 512), BF),
            V((2, 512, 128), BF),
            V((2, 128, 512), BF),
            V((64, 128), F32),
            V((128, 128), F32),
            V((512, 256), F32),
            V((512, 256), F32),
            V((512, 256), F32),
            V((512, 256), F32),
            V((512, 256), F32),
            V((512, 256), F32),
            V((512, 256), BF),
            V((FILTER_DEG + 1, 128, 256), BF),
            V((FILTER_DEG + 1, 128, 256), BF),
            V((8, 2, 512, 256), BF),
            V((512, 512), BF),
            V((8, 2, 4, 2, 64, 256), BF),
            V((8, 2, 2, 64, 256), BF),
            V((8, 2, 2, 2, 64, 256), BF),
            V((8, 2, 4, 2, 16, 256), BF),
            V((8, 2, 2, 16, 256), BF),
            V((8, 2, 2, 2, 16, 256), BF),
            V((8, 2, 2, 16, 256), F32),
            V((2, 256, 512), BF),
            dma((4,)),
            dma((4,)),
            dma((4,)),
            dma,
            dma,
            dma((FILTER_DEG + 1, 2)),
            dma((FILTER_DEG + 1, 2)),
            dma((2, 7)),
            dma((2, 7)),
            dma((8, 2)),
            dma((8, 2)),
            dma((8, 2, 2, 4)),
            dma((8, 2, 2, 4)),
        ],
        compiler_params=pltpu.CompilerParams(
            collective_id=0, has_side_effects=True, vmem_limit_bytes=56 * 1024 * 1024
        ),
    )(
        orbital_block,
        cell_matrices,
        cell_nodes.T,
        shared_nodes,
        inv_sqrt_mass.reshape(1, 256),
        potential.reshape(1, 256),
        filter_center,
        filter_halfwidth,
    )


def solution(mesh):
    return jax.shard_map(
        shards,
        mesh=mesh,
        in_specs=(
            P("dom", "band"),
            P("dom", None, None),
            P(None, "dom"),
            P("dom", None),
            P("dom"),
            P("dom"),
            P(),
            P(),
        ),
        out_specs=(P("dom", "band"), P(("band", "dom"), None), P(("band", "dom"), None)),
        check_vma=False,
    )
```

```python
import jax
import jax.numpy as jnp
from jax import lax
from jax.experimental import pallas as pl
from jax.experimental.pallas import tpu as pltpu
from jax.sharding import PartitionSpec as P

FILTER_DEG = 4
BF = jnp.bfloat16
F32 = jnp.float32
MESH = pl.DeviceIdType.MESH
ORDER = (0, 7, 1, 6, 2, 5, 3, 4)


def nn(a, b):
    return lax.dot_general(a, b, (((1,), (0,)), ((), ())), preferred_element_type=F32)


def nt(a, b):
    return lax.dot_general(a, b, (((1,), (1,)), ((), ())), preferred_element_type=F32)


def split(a):
    hi = a.astype(BF)
    return hi, (a - hi.astype(F32)).astype(BF)


def rows_equal(count, row, base=0):
    index = lax.broadcasted_iota(jnp.int32, (count, row.shape[1]), 0) + base
    return jnp.where(index == row, 1.0, 0.0).astype(BF)


def kernel(
    x_ref, m_ref, nodes_ref, shared_ref, mass_ref, pot_ref, center_ref, half_ref,
    filt_ref, inter_ref, proj_ref,
    mown, ints_own, vecs_own, xp, xc, m2, ints2, vecs2, perm,
    gt0, u0, gt1, u1, kmat, k1, ahi, alo, w2, wc, q0, eye, kgg_out, kgg_in,
    invb, invl, potb, potl, vcur, vprev, sbuf, gc_out, gc_in,
    fall, fat, p1, r1a, r1b, p2, r2a, r2b, sfin, fin,
    loc_sem, set_s, set_r, kgg_s, kgg_r, halo_s, halo_r,
    zs, zr, cs, cr, rs_s, rs_r,
):
    band = lax.axis_index("band")
    dom = lax.axis_index("dom")
    zh, core = band // 2, band % 2
    zl, x, y = dom % 2, (dom // 2) % 4, dom // 8
    z = zh * 2 + zl

    def device(zz, yy, xx, cc):
        return ((zz // 2) * 2 + cc, (yy * 4 + xx) * 2 + zz % 2)

    z_up, z_down = device((z + 1) % 8, y, x, core), device((z + 7) % 8, y, x, core)
    x_up, x_down = device(z, y, (x + 1) % 4, core), device(z, y, (x + 3) % 4, core)
    y_up, y_down = device(z, (y + 1) % 4, x, core), device(z, (y + 3) % 4, x, core)
    mate = device(z, y, x, 1 - core)
    pair = device(zh * 2 + 1 - zl, y, x, core)
    slab = y * 4 + x
    after, before = (slab + 1) % 16, (slab + 15) % 16
    nxt = device(z, after // 4, after % 4, core)
    prv = device(z, before // 4, before % 4, core)

    barrier = pltpu.get_barrier_semaphore()
    friends = (z_up, z_down, x_up, x_down, y_up, y_down, mate, nxt, prv)
    for friend in friends:
        pl.semaphore_signal(barrier, inc=1, device_id=friend, device_id_type=MESH)

    def send(src, dst, ssem, rsem, to):
        copy = pltpu.make_async_remote_copy(
            src_ref=src, dst_ref=dst, send_sem=ssem, recv_sem=rsem,
            device_id=to, device_id_type=MESH,
        )
        copy.start()
        return copy

    started = []

    ints_own[...] = jnp.full((8, 128), -1, jnp.int32)
    ints_own[0:4, 0:125] = nodes_ref[...]
    ints_own[4:5, 0:64] = shared_ref[...]
    ints_own[5:6, 64:128] = shared_ref[...]
    vecs_own[...] = jnp.zeros_like(vecs_own)
    vecs_own[0:1] = mass_ref[...]
    vecs_own[1:2] = pot_ref[...]
    mown[...] = jnp.zeros_like(mown)
    for c in range(4):
        mown[c, 0:125, 0:125] = m_ref[:, c, :]
    kgg_in[64:128] = jnp.zeros((64, 128), F32)

    cells = pl.ds(core * 2, 2)
    pl.semaphore_wait(barrier, len(friends))
    setup = [
        send(ints_own, ints2.at[zl], set_s.at[0], set_r.at[0], pair),
        send(vecs_own, vecs2.at[zl], set_s.at[1], set_r.at[1], pair),
        send(mown.at[cells], m2.at[zl, cells], set_s.at[2], set_r.at[2], pair),
    ]
    own = [
        pltpu.make_async_copy(ints_own, ints2.at[zl], loc_sem.at[0]),
        pltpu.make_async_copy(vecs_own, vecs2.at[zl], loc_sem.at[1]),
        pltpu.make_async_copy(mown, m2.at[zl], loc_sem.at[2]),
    ]
    for copy in own:
        copy.start()
    col = lax.broadcasted_iota(jnp.int32, (512, 512), 0)
    place = lax.broadcasted_iota(jnp.int32, (512, 512), 1)
    goal = ((col >> 4) & 1) * 256 + (col >> 5) * 16 + (col & 15)
    perm[...] = jnp.where(goal == place, 1.0, 0.0).astype(BF)
    for half in range(2):
        xp[half] = nn(x_ref[...], perm[:, half * 256 : half * 256 + 256]).astype(BF)
    setup.append(send(xp.at[1 - zl], xc.at[zl], set_s.at[3], set_r.at[3], pair))
    own.append(pltpu.make_async_copy(xp.at[zl], xc.at[zl], loc_sem.at[3]))
    own[3].start()
    started += setup
    for copy in own[0:2]:
        copy.wait()
    for copy in setup[0:2]:
        copy.wait_recv()

    q1t = rows_equal(256, ints2[1, 4:5, :])
    q0t = rows_equal(256, ints2[0, 4:5, :])
    q0t_right = rows_equal(256, ints2[0, 5:6, :])
    for c in range(4):
        lanes = slice(c * 128, c * 128 + 128)
        row = ints2[0, c : c + 1, :]
        top = rows_equal(256, row)
        ghost = rows_equal(128, row, 256)
        bottom = nn(q1t, ghost).astype(BF)
        gt0[0:256, lanes] = top
        gt0[256:512, lanes] = bottom
        gt1[:, lanes] = rows_equal(384, ints2[1, c : c + 1, :])
    setup[2].wait_recv()
    half_cells = m2.at[1 - zl, cells]
    shared_cells = send(half_cells, half_cells, set_s.at[4], set_r.at[4], mate)
    started.append(shared_cells)
    own[2].wait()
    shared_cells.wait_recv()
    for c in range(4):
        lanes = slice(c * 128, c * 128 + 128)
        u1[:, lanes] = nn(gt1[:, lanes], m2[1, c]).astype(BF)
    for c in range(4):
        lanes = slice(c * 128, c * 128 + 128)
        u0[:, lanes] = nn(gt0[:, lanes], m2[0, c]).astype(BF)
    k1[...] = nt(u1[...], gt1[...])
    kgg_out[...] = k1[256:320, 256:384]
    kgg = send(kgg_out, kgg_in.at[0:64], kgg_s, kgg_r, nxt)
    started.append(kgg)
    kmat[...] = nt(u0[...], gt0[...])
    kmat[256:512, 256:512] += k1[0:256, 0:256]
    w2[0, 0:256] = q0t_right
    hi, lo = split(k1[0:256, 256:384])
    w2[0, 256:512] = hi
    w2[1, 256:512] = lo
    unit = lax.broadcasted_iota(jnp.int32, (256, 256), 0)
    eye[...] = jnp.where(unit == lax.broadcasted_iota(jnp.int32, (256, 256), 1), 1.0, 0.0).astype(BF)
    q0[...] = nt(eye[0:128, 0:128], q0t_right)[64:128].astype(BF)
    hi, lo = split(k1[256:320, 0:256])
    wc[0] = hi
    wc[1] = lo

    center, halfwidth = center_ref[0], half_ref[0]
    own[3].wait()
    setup[3].wait_recv()
    for slot in range(2):
        nodes = slice(slot * 256, slot * 256 + 256)
        columns = jnp.transpose(vecs2[slot])
        mass = jnp.broadcast_to(columns[:, 0:1], (256, 256))
        pot = jnp.broadcast_to(columns[:, 1:2], (256, 256))
        invb[nodes] = mass
        potb[nodes] = pot
        invl[nodes] = mass / halfwidth
        potl[nodes] = (pot - center) / halfwidth
        start = xc[slot].astype(F32)
        vcur[nodes] = start
        sbuf[nodes] = (mass * start).astype(BF)

    def push(step, half):
        if half == 1:
            out = nn(wc[0], sbuf[256:512]) + nn(wc[1], sbuf[256:512])
            rows, landing, to = slice(0, 64), slice(64, 128), nxt
        else:
            out = nn(q0[...], sbuf[0:256])
            rows, landing, to = slice(64, 128), slice(0, 64), prv
        gc_out[step, rows] = out.astype(BF)
        copy = send(
            gc_out.at[step, rows], gc_in.at[step, landing],
            halo_s.at[step, half], halo_r.at[step, half], to,
        )
        started.append(copy)
        return copy

    def inside():
        return nn(ahi[...], sbuf[...]) + nn(alo[...], sbuf[...])

    def whole(inner, half, came):
        nodes = slice(half * 256, half * 256 + 256)
        total = inner[nodes] + nn(w2[0, nodes], came)
        if half == 1:
            total = total + nn(w2[1, nodes], came)
        return nodes, total

    copies = [push(0, 1), push(0, 0)]
    kgg.wait_recv()
    hi, lo = split(kgg_in[...])
    hi, lo = split(nn(q0t, hi) + nn(q0t, lo))
    kmat[0:256, 0:256] += nt(hi, q0t) + nt(lo, q0t)
    hi, lo = split(kmat[...])
    ahi[...] = hi
    alo[...] = lo

    for step in range(FILTER_DEG):
        inner = inside()
        for copy in copies:
            copy.wait_recv()
        came = gc_in[step]
        copies = []
        for half in (1, 0):
            nodes, total = whole(inner, half, came)
            image = invl[nodes] * total + potl[nodes] * vcur[nodes]
            if step > 0:
                image = 2.0 * image - vprev[nodes]
            if step < FILTER_DEG - 1:
                vprev[nodes] = vcur[nodes]
            else:
                filtered = image.astype(BF)
                fall[0, core, nodes] = filtered
                image = filtered.astype(F32)
            vcur[nodes] = image
            sbuf[nodes] = (invb[nodes] * image).astype(BF)
            copies.append(push(step + 1, half))

    tours = ([], [])

    def onward(way, slot, half):
        landing = (slot + 7) % 8 if way == 0 else (slot + 1) % 8
        nodes = slice(half * 128, half * 128 + 128)
        number = len(tours[way])
        copy = send(
            fall.at[slot, core, nodes], fall.at[landing, core, nodes],
            zs.at[way, number], zr.at[way, number], (z_up, z_down)[way],
        )
        tours[way].append((copy, landing, half))
        started.append(copy)

    others = {}

    def across(slot, half):
        block = fall.at[slot, core, half * 128 : half * 128 + 128]
        others[slot, half] = send(block, block, cs.at[slot, half], cr.at[slot, half], mate)
        started.append(others[slot, half])

    def arrive(number):
        for way in range(2):
            copy, slot, half = tours[way][number]
            copy.wait_recv()
            if number < 10:
                onward(way, slot, half)
            across(slot, half)

    for half in range(4):
        onward(0, 0, half)
        onward(1, 0, 3 - half)
        across(0, half)

    lines = (((x, x_up, x_down), (y, y_up, y_down)), ((y, y_up, y_down), (x, x_up, x_down)))
    flights = {}

    def ring_first(piece, mat, level):
        pos, right, left = lines[mat ^ (piece & 1)][level]
        part, in_a = (p1, r1a) if level == 0 else (p2, r2a)
        far = (pos + 2) % 4
        sem = (piece, mat, level)
        pairs = []
        for side, to in ((0, right), (1, left)):
            pairs.append(send(
                part.at[piece, mat, far, side], in_a.at[piece, mat, side],
                rs_s.at[(*sem, side)], rs_r.at[(*sem, side)], to,
            ))
        flights[(*sem, 0)] = pairs
        started.extend(pairs)

    def ring_second(piece, mat, level):
        pos, right, left = lines[mat ^ (piece & 1)][level]
        part, in_a, in_b = (p1, r1a, r1b) if level == 0 else (p2, r2a, r2b)
        sem = (piece, mat, level)
        pairs = []
        for side, to in ((0, right), (1, left)):
            near = (pos + 1) % 4 if side == 0 else (pos + 3) % 4
            flights[(*sem, 0)][side].wait_recv()
            whole = part[piece, mat, near, side].astype(F32) + in_a[piece, mat, side].astype(F32)
            part[piece, mat, near, side] = whole.astype(BF)
            pairs.append(send(
                part.at[piece, mat, near], in_b.at[piece, mat, side],
                rs_s.at[(*sem, 2 + side)], rs_r.at[(*sem, 2 + side)], to,
            ))
        flights[(*sem, 1)] = pairs
        started.extend(pairs)

    def ring_last(piece, mat, level):
        pos, right, left = lines[mat ^ (piece & 1)][level]
        part, in_b = (p1, r1b) if level == 0 else (p2, r2b)
        for copy in flights[(piece, mat, level, 1)]:
            copy.wait_recv()
        return (
            part[piece, mat, pos].astype(F32)
            + in_b[piece, mat, 0].astype(F32)
            + in_b[piece, mat, 1].astype(F32)
        )

    def place(product, piece, mat, side):
        for yy in range(4):
            k = yy * 64
            if mat ^ (piece & 1):
                p1[piece, mat, yy, side] = product[k : k + 64]
            else:
                for xx in range(4):
                    rows = product[k + xx * 16 : k + xx * 16 + 16]
                    p1[piece, mat, xx, side, yy * 16 : yy * 16 + 16] = rows

    def landed(slot):
        for part in range(4):
            others[slot, part].wait_recv()

    def stage(number, piece):
        slot = ORDER[piece]
        if number == 0:
            for turn in range(2):
                side = core if turn == 0 else 1 - core
                if turn == 1:
                    landed(slot)
                product = nn(fat[...], fall[slot, side]).astype(BF)
                for mat in range(2):
                    place(product[mat * 256 : mat * 256 + 256], piece, mat, side)
            for mat in range(2):
                ring_first(piece, mat, 0)
        elif number == 1:
            for mat in range(2):
                ring_second(piece, mat, 0)
        elif number == 2:
            for mat in range(2):
                level_sum = ring_last(piece, mat, 0).astype(BF)
                for to in range(4):
                    p2[piece, mat, to] = level_sum[:, to * 16 : to * 16 + 16]
                ring_first(piece, mat, 1)
        elif number == 3:
            for mat in range(2):
                ring_second(piece, mat, 1)
        else:
            source = (z + slot) % 8
            for mat in range(2):
                sfin[source, :, mat] = ring_last(piece, mat, 1)

    inner = inside()
    fat[0:256] = nt(eye[...], fall[0, core]).astype(BF)
    place(nn(fat[0:256], fall[0, core]).astype(BF), 0, 0, core)
    landed(0)
    place(nn(fat[0:256], fall[0, 1 - core]).astype(BF), 0, 0, 1 - core)
    ring_first(0, 0, 0)
    arrive(0)
    for copy in copies:
        copy.wait_recv()
    came = gc_in[FILTER_DEG]
    for half in (1, 0):
        nodes, total = whole(inner, half, came)
        sbuf[nodes] = (invb[nodes] * total + potb[nodes] * vcur[nodes]).astype(BF)
    arrive(1)
    fat[256:512] = nt(eye[...], sbuf[...]).astype(BF)
    for side in range(2):
        place(nn(fat[256:512], fall[0, side]).astype(BF), 0, 1, side)
    ring_first(0, 1, 0)
    arrive(2)

    ahead = {1: (3,), 3: (7,), 5: (11,)}
    behind = {1: (4,), 2: (5, 6), 3: (8,), 4: (9, 10), 5: (12,), 6: (13,)}
    for tick in range(1, 16):
        for number in ahead.get(tick, ()):
            arrive(number)
        for number in range(4, -1, -1):
            piece = tick - 2 * number
            if 0 <= piece < 8:
                stage(number, piece)
        for number in behind.get(tick, ()):
            arrive(number)
        if tick == 8:
            mine = pl.ds(pl.multiple_of(zl * 256, 256), 256)
            filt_ref[...] = nt(fall[zl * 7, core, mine], perm[:, 0:256]) + nt(
                fall[1 - zl, core, mine], perm[:, 256:512]
            )

    for group in range(8):
        lines_of = slice(group * 32, group * 32 + 32)
        for half in range(2):
            block = sfin[(group // 2) * 2 + half, group % 2].reshape(32, 256)
            hi, lo = split(block)
            fin[0, lines_of, half * 256 : half * 256 + 256] = hi
            fin[1, lines_of, half * 256 : half * 256 + 256] = lo
    result = nt(fin[0], perm[...]) + nt(fin[1], perm[...])
    for group in range(8):
        lanes = slice(group * 512, group * 512 + 512)
        inter_ref[:, lanes] = result[group * 32 : group * 32 + 16]
        proj_ref[:, lanes] = result[group * 32 + 16 : group * 32 + 32]
    for copy in started:
        copy.wait_send()


def shards(
    orbital_block,
    cell_matrices,
    cell_nodes,
    shared_nodes,
    inv_sqrt_mass,
    potential,
    filter_center,
    filter_halfwidth,
):
    vm = pl.BlockSpec(memory_space=pltpu.VMEM)
    sm = pl.BlockSpec(memory_space=pltpu.SMEM)
    V = pltpu.VMEM
    dma = pltpu.SemaphoreType.DMA
    filtered, intersection, projected = pl.pallas_call(
        kernel,
        out_shape=(
            jax.ShapeDtypeStruct((256, 512), F32),
            jax.ShapeDtypeStruct((16, 4096), F32),
            jax.ShapeDtypeStruct((16, 4096), F32),
        ),
        in_specs=[vm, vm, vm, vm, vm, vm, sm, sm],
        out_specs=(vm, vm, vm),
        scratch_shapes=[
            V((4, 128, 128), BF),
            V((8, 128), jnp.int32),
            V((8, 256), F32),
            V((2, 256, 256), BF),
            V((2, 256, 256), BF),
            V((2, 4, 128, 128), BF),
            V((2, 8, 128), jnp.int32),
            V((2, 8, 256), F32),
            V((512, 512), BF),
            V((512, 512), BF),
            V((512, 512), BF),
            V((384, 512), BF),
            V((384, 512), BF),
            V((512, 512), F32),
            V((384, 384), F32),
            V((512, 512), BF),
            V((512, 512), BF),
            V((2, 512, 128), BF),
            V((2, 64, 256), BF),
            V((64, 256), BF),
            V((256, 256), BF),
            V((64, 128), F32),
            V((128, 128), F32),
            V((512, 256), F32),
            V((512, 256), F32),
            V((512, 256), F32),
            V((512, 256), F32),
            V((512, 256), F32),
            V((512, 256), F32),
            V((512, 256), BF),
            V((FILTER_DEG + 1, 128, 256), BF),
            V((FILTER_DEG + 1, 128, 256), BF),
            V((8, 2, 512, 256), BF),
            V((512, 512), BF),
            V((8, 2, 4, 2, 64, 256), BF),
            V((8, 2, 2, 64, 256), BF),
            V((8, 2, 2, 2, 64, 256), BF),
            V((8, 2, 4, 2, 16, 256), BF),
            V((8, 2, 2, 16, 256), BF),
            V((8, 2, 2, 2, 16, 256), BF),
            V((8, 2, 2, 16, 256), F32),
            V((2, 256, 512), BF),
            dma((4,)),
            dma((5,)),
            dma((5,)),
            dma,
            dma,
            dma((FILTER_DEG + 1, 2)),
            dma((FILTER_DEG + 1, 2)),
            dma((2, 14)),
            dma((2, 14)),
            dma((8, 4)),
            dma((8, 4)),
            dma((8, 2, 2, 4)),
            dma((8, 2, 2, 4)),
        ],
        compiler_params=pltpu.CompilerParams(
            collective_id=0, has_side_effects=True, vmem_limit_bytes=56 * 1024 * 1024
        ),
    )(
        orbital_block,
        jnp.transpose(cell_matrices, (1, 0, 2)),
        cell_nodes.T,
        shared_nodes,
        inv_sqrt_mass.reshape(1, 256),
        potential.reshape(1, 256),
        filter_center,
        filter_halfwidth,
    )
    factor = 1.0 / 8192
    return filtered.astype(BF), intersection * factor, projected * factor


def solution(mesh):
    return jax.shard_map(
        shards,
        mesh=mesh,
        in_specs=(
            P("dom", "band"),
            P("dom", None, None),
            P(None, "dom"),
            P("dom", None),
            P("dom"),
            P("dom"),
            P(),
            P(),
        ),
        out_specs=(P("dom", "band"), P(("band", "dom"), None), P(("band", "dom"), None)),
        check_vma=False,
    )
```

```python
import jax
import jax.numpy as jnp
from jax import lax
from jax.experimental import pallas as pl
from jax.experimental.pallas import tpu as pltpu
from jax.sharding import PartitionSpec as P

FILTER_DEG = 4
BF = jnp.bfloat16
F32 = jnp.float32
MESH = pl.DeviceIdType.MESH
ORDER = (0, 7, 1, 6, 2, 5, 3, 4)


def nn(a, b):
    return lax.dot_general(a, b, (((1,), (0,)), ((), ())), preferred_element_type=F32)


def nt(a, b):
    return lax.dot_general(a, b, (((1,), (1,)), ((), ())), preferred_element_type=F32)


def split(a):
    hi = a.astype(BF)
    return hi, (a - hi.astype(F32)).astype(BF)


def rows_equal(count, row, base=0):
    index = lax.broadcasted_iota(jnp.int32, (count, row.shape[1]), 0) + base
    return jnp.where(index == row, 1.0, 0.0).astype(BF)


def kernel(
    x_hbm, m_hbm, nodes_hbm, shared_hbm, mass_hbm, pot_hbm, center_ref, half_ref,
    filt_ref, inter_ref, proj_ref,
    x_ref, m_ref, nodes_ref, shared_ref, mass_ref, pot_ref, mown, ints_own, vecs_own, xp, xc, m2, ints2, vecs2, perm,
    gt0, u0, gt1, u1, kmat, k1, ahi, alo, w2, wc, q0, eye, kgg_out, kgg_in,
    invb, invl, potb, potl, vcur, vprev, sbuf, gc_out, gc_in,
    fall, fat, p1, r1a, r1b, p2, r2a, r2b, sfin, fin,
    loc_sem, set_s, set_r, kgg_s, kgg_r, halo_s, halo_r,
    zs, zr, cs, cr, rs_s, rs_r,
):
    band = lax.axis_index("band")
    dom = lax.axis_index("dom")
    zh, core = band // 2, band % 2
    zl, x, y = dom % 2, (dom // 2) % 4, dom // 8
    z = zh * 2 + zl

    def device(zz, yy, xx, cc):
        return ((zz // 2) * 2 + cc, (yy * 4 + xx) * 2 + zz % 2)

    z_up, z_down = device((z + 1) % 8, y, x, core), device((z + 7) % 8, y, x, core)
    x_up, x_down = device(z, y, (x + 1) % 4, core), device(z, y, (x + 3) % 4, core)
    y_up, y_down = device(z, (y + 1) % 4, x, core), device(z, (y + 3) % 4, x, core)
    mate = device(z, y, x, 1 - core)
    pair = device(zh * 2 + 1 - zl, y, x, core)
    slab = y * 4 + x
    after, before = (slab + 1) % 16, (slab + 15) % 16
    nxt = device(z, after // 4, after % 4, core)
    prv = device(z, before // 4, before % 4, core)

    barrier = pltpu.get_barrier_semaphore()
    friends = (z_up, z_down, x_up, x_down, y_up, y_down, mate, nxt, prv)
    for friend in friends:
        pl.semaphore_signal(barrier, inc=1, device_id=friend, device_id_type=MESH)

    def send(src, dst, ssem, rsem, to):
        copy = pltpu.make_async_remote_copy(
            src_ref=src, dst_ref=dst, send_sem=ssem, recv_sem=rsem,
            device_id=to, device_id_type=MESH,
        )
        copy.start()
        return copy

    started = []

    brought = [
        pltpu.make_async_copy(src, dst, loc_sem.at[4 + number])
        for number, (src, dst) in enumerate((
            (nodes_hbm, nodes_ref), (shared_hbm, shared_ref), (mass_hbm, mass_ref),
            (pot_hbm, pot_ref), (m_hbm, m_ref), (x_hbm, x_ref),
        ))
    ]
    for copy in brought:
        copy.start()
    ints_own[...] = jnp.full((8, 128), -1, jnp.int32)
    vecs_own[...] = jnp.zeros_like(vecs_own)
    mown[...] = jnp.zeros_like(mown)
    kgg_in[64:128] = jnp.zeros((64, 128), F32)
    for copy in brought[0:4]:
        copy.wait()
    ints_own[0:4, 0:125] = nodes_ref[...]
    ints_own[4:5, 0:64] = shared_ref[...]
    ints_own[5:6, 64:128] = shared_ref[...]
    vecs_own[0:1] = mass_ref[...]
    vecs_own[1:2] = pot_ref[...]
    brought[4].wait()
    for c in range(4):
        mown[c, 0:125, 0:125] = m_ref[:, c, :]
    cells = pl.ds(core * 2, 2)
    pl.semaphore_wait(barrier, len(friends))
    setup = [
        send(ints_own, ints2.at[zl], set_s.at[0], set_r.at[0], pair),
        send(vecs_own, vecs2.at[zl], set_s.at[1], set_r.at[1], pair),
        send(mown.at[cells], m2.at[zl, cells], set_s.at[2], set_r.at[2], pair),
    ]
    own = [
        pltpu.make_async_copy(ints_own, ints2.at[zl], loc_sem.at[0]),
        pltpu.make_async_copy(vecs_own, vecs2.at[zl], loc_sem.at[1]),
        pltpu.make_async_copy(mown, m2.at[zl], loc_sem.at[2]),
    ]
    for copy in own:
        copy.start()
    brought[5].wait()
    col = lax.broadcasted_iota(jnp.int32, (512, 512), 0)
    place = lax.broadcasted_iota(jnp.int32, (512, 512), 1)
    goal = ((col >> 4) & 1) * 256 + (col >> 5) * 16 + (col & 15)
    perm[...] = jnp.where(goal == place, 1.0, 0.0).astype(BF)
    for half in range(2):
        xp[half] = nn(x_ref[...], perm[:, half * 256 : half * 256 + 256]).astype(BF)
    setup.append(send(xp.at[1 - zl], xc.at[zl], set_s.at[3], set_r.at[3], pair))
    own.append(pltpu.make_async_copy(xp.at[zl], xc.at[zl], loc_sem.at[3]))
    own[3].start()
    started += setup
    for copy in own[0:2]:
        copy.wait()
    for copy in setup[0:2]:
        copy.wait_recv()

    q1t = rows_equal(256, ints2[1, 4:5, :])
    q0t = rows_equal(256, ints2[0, 4:5, :])
    q0t_right = rows_equal(256, ints2[0, 5:6, :])
    for c in range(4):
        lanes = slice(c * 128, c * 128 + 128)
        row = ints2[0, c : c + 1, :]
        top = rows_equal(256, row)
        ghost = rows_equal(128, row, 256)
        bottom = nn(q1t, ghost).astype(BF)
        gt0[0:256, lanes] = top
        gt0[256:512, lanes] = bottom
        gt1[:, lanes] = rows_equal(384, ints2[1, c : c + 1, :])
    setup[2].wait_recv()
    half_cells = m2.at[1 - zl, cells]
    shared_cells = send(half_cells, half_cells, set_s.at[4], set_r.at[4], mate)
    started.append(shared_cells)
    own[2].wait()
    shared_cells.wait_recv()
    for c in range(4):
        lanes = slice(c * 128, c * 128 + 128)
        u1[:, lanes] = nn(gt1[:, lanes], m2[1, c]).astype(BF)
    for c in range(4):
        lanes = slice(c * 128, c * 128 + 128)
        u0[:, lanes] = nn(gt0[:, lanes], m2[0, c]).astype(BF)
    k1[...] = nt(u1[...], gt1[...])
    kgg_out[...] = k1[256:320, 256:384]
    kgg = send(kgg_out, kgg_in.at[0:64], kgg_s, kgg_r, nxt)
    started.append(kgg)
    kmat[...] = nt(u0[...], gt0[...])
    kmat[256:512, 256:512] += k1[0:256, 0:256]
    w2[0, 0:256] = q0t_right
    hi, lo = split(k1[0:256, 256:384])
    w2[0, 256:512] = hi
    w2[1, 256:512] = lo
    unit = lax.broadcasted_iota(jnp.int32, (256, 256), 0)
    eye[...] = jnp.where(unit == lax.broadcasted_iota(jnp.int32, (256, 256), 1), 1.0, 0.0).astype(BF)
    q0[...] = nt(eye[0:128, 0:128], q0t_right)[64:128].astype(BF)
    hi, lo = split(k1[256:320, 0:256])
    wc[0] = hi
    wc[1] = lo

    center, halfwidth = center_ref[0], half_ref[0]
    own[3].wait()
    setup[3].wait_recv()
    for slot in range(2):
        nodes = slice(slot * 256, slot * 256 + 256)
        columns = jnp.transpose(vecs2[slot])
        mass = jnp.broadcast_to(columns[:, 0:1], (256, 256))
        pot = jnp.broadcast_to(columns[:, 1:2], (256, 256))
        invb[nodes] = mass
        potb[nodes] = pot
        invl[nodes] = mass / halfwidth
        potl[nodes] = (pot - center) / halfwidth
        start = xc[slot].astype(F32)
        vcur[nodes] = start
        sbuf[nodes] = (mass * start).astype(BF)

    def push(step, half):
        if half == 1:
            out = nn(wc[0], sbuf[256:512]) + nn(wc[1], sbuf[256:512])
            rows, landing, to = slice(0, 64), slice(64, 128), nxt
        else:
            out = nn(q0[...], sbuf[0:256])
            rows, landing, to = slice(64, 128), slice(0, 64), prv
        gc_out[step, rows] = out.astype(BF)
        copy = send(
            gc_out.at[step, rows], gc_in.at[step, landing],
            halo_s.at[step, half], halo_r.at[step, half], to,
        )
        started.append(copy)
        return copy

    def inside():
        return nn(ahi[...], sbuf[...]) + nn(alo[...], sbuf[...])

    def whole(inner, half, came):
        nodes = slice(half * 256, half * 256 + 256)
        total = inner[nodes] + nn(w2[0, nodes], came)
        if half == 1:
            total = total + nn(w2[1, nodes], came)
        return nodes, total

    copies = [push(0, 1), push(0, 0)]
    kgg.wait_recv()
    hi, lo = split(kgg_in[...])
    hi, lo = split(nn(q0t, hi) + nn(q0t, lo))
    kmat[0:256, 0:256] += nt(hi, q0t) + nt(lo, q0t)
    hi, lo = split(kmat[...])
    ahi[...] = hi
    alo[...] = lo

    for step in range(FILTER_DEG):
        inner = inside()
        for copy in copies:
            copy.wait_recv()
        came = gc_in[step]
        copies = []
        for half in (1, 0):
            nodes, total = whole(inner, half, came)
            image = invl[nodes] * total + potl[nodes] * vcur[nodes]
            if step > 0:
                image = 2.0 * image - vprev[nodes]
            if step < FILTER_DEG - 1:
                vprev[nodes] = vcur[nodes]
            else:
                filtered = image.astype(BF)
                fall[0, core, nodes] = filtered
                image = filtered.astype(F32)
            vcur[nodes] = image
            sbuf[nodes] = (invb[nodes] * image).astype(BF)
            copies.append(push(step + 1, half))

    tours = ([], [])

    def onward(way, slot, half):
        landing = (slot + 7) % 8 if way == 0 else (slot + 1) % 8
        nodes = slice(half * 128, half * 128 + 128)
        number = len(tours[way])
        copy = send(
            fall.at[slot, core, nodes], fall.at[landing, core, nodes],
            zs.at[way, number], zr.at[way, number], (z_up, z_down)[way],
        )
        tours[way].append((copy, landing, half))
        started.append(copy)

    others, pieces_in = {}, {}

    def across(slot, half):
        pieces_in[slot] = pieces_in.get(slot, 0) + 1
        if pieces_in[slot] == 4:
            block = fall.at[slot, core]
            others[slot] = send(block, block, cs.at[slot, 0], cr.at[slot, 0], mate)
            started.append(others[slot])

    def arrive(number):
        for way in range(2):
            copy, slot, half = tours[way][number]
            copy.wait_recv()
            if number < 10:
                onward(way, slot, half)
            across(slot, half)

    for half in range(4):
        onward(0, 0, half)
        onward(1, 0, 3 - half)
        across(0, half)

    lines = (((x, x_up, x_down), (y, y_up, y_down)), ((y, y_up, y_down), (x, x_up, x_down)))
    flights = {}

    def ring_first(piece, mat, level):
        pos, right, left = lines[mat ^ (piece & 1)][level]
        part, in_a = (p1, r1a) if level == 0 else (p2, r2a)
        far = (pos + 2) % 4
        sem = (piece, mat, level)
        pairs = []
        for side, to in ((0, right), (1, left)):
            pairs.append(send(
                part.at[piece, mat, far, side], in_a.at[piece, mat, side],
                rs_s.at[(*sem, side)], rs_r.at[(*sem, side)], to,
            ))
        flights[(*sem, 0)] = pairs
        started.extend(pairs)

    def ring_second(piece, mat, level):
        pos, right, left = lines[mat ^ (piece & 1)][level]
        part, in_a, in_b = (p1, r1a, r1b) if level == 0 else (p2, r2a, r2b)
        sem = (piece, mat, level)
        pairs = []
        for side, to in ((0, right), (1, left)):
            near = (pos + 1) % 4 if side == 0 else (pos + 3) % 4
            flights[(*sem, 0)][side].wait_recv()
            whole = part[piece, mat, near, side].astype(F32) + in_a[piece, mat, side].astype(F32)
            part[piece, mat, near, side] = whole.astype(BF)
            pairs.append(send(
                part.at[piece, mat, near], in_b.at[piece, mat, side],
                rs_s.at[(*sem, 2 + side)], rs_r.at[(*sem, 2 + side)], to,
            ))
        flights[(*sem, 1)] = pairs
        started.extend(pairs)

    def ring_last(piece, mat, level):
        pos, right, left = lines[mat ^ (piece & 1)][level]
        part, in_b = (p1, r1b) if level == 0 else (p2, r2b)
        for copy in flights[(piece, mat, level, 1)]:
            copy.wait_recv()
        return (
            part[piece, mat, pos].astype(F32)
            + in_b[piece, mat, 0].astype(F32)
            + in_b[piece, mat, 1].astype(F32)
        )

    def place(product, piece, mat, side):
        for yy in range(4):
            k = yy * 64
            if mat ^ (piece & 1):
                p1[piece, mat, yy, side] = product[k : k + 64]
            else:
                for xx in range(4):
                    rows = product[k + xx * 16 : k + xx * 16 + 16]
                    p1[piece, mat, xx, side, yy * 16 : yy * 16 + 16] = rows

    def landed(slot):
        others[slot].wait_recv()

    def stage(number, piece):
        slot = ORDER[piece]
        if number == 0:
            for turn in range(2):
                side = core if turn == 0 else 1 - core
                if turn == 1:
                    landed(slot)
                product = nn(fat[...], fall[slot, side]).astype(BF)
                for mat in range(2):
                    place(product[mat * 256 : mat * 256 + 256], piece, mat, side)
            for mat in range(2):
                ring_first(piece, mat, 0)
        elif number == 1:
            for mat in range(2):
                ring_second(piece, mat, 0)
        elif number == 2:
            for mat in range(2):
                level_sum = ring_last(piece, mat, 0).astype(BF)
                for to in range(4):
                    p2[piece, mat, to] = level_sum[:, to * 16 : to * 16 + 16]
                ring_first(piece, mat, 1)
        elif number == 3:
            for mat in range(2):
                ring_second(piece, mat, 1)
        else:
            source = (z + slot) % 8
            for mat in range(2):
                sfin[source, :, mat] = ring_last(piece, mat, 1)

    inner = inside()
    fat[0:256] = nt(eye[...], fall[0, core]).astype(BF)
    place(nn(fat[0:256], fall[0, core]).astype(BF), 0, 0, core)
    landed(0)
    place(nn(fat[0:256], fall[0, 1 - core]).astype(BF), 0, 0, 1 - core)
    ring_first(0, 0, 0)
    arrive(0)
    for copy in copies:
        copy.wait_recv()
    came = gc_in[FILTER_DEG]
    for half in (1, 0):
        nodes, total = whole(inner, half, came)
        sbuf[nodes] = (invb[nodes] * total + potb[nodes] * vcur[nodes]).astype(BF)
    arrive(1)
    fat[256:512] = nt(eye[...], sbuf[...]).astype(BF)
    for side in range(2):
        place(nn(fat[256:512], fall[0, side]).astype(BF), 0, 1, side)
    ring_first(0, 1, 0)
    arrive(2)

    ahead = {1: (3,), 3: (7,), 5: (11,)}
    behind = {1: (4,), 2: (5, 6), 3: (8,), 4: (9, 10), 5: (12,), 6: (13,)}
    for tick in range(1, 16):
        for number in ahead.get(tick, ()):
            arrive(number)
        for number in range(4, -1, -1):
            piece = tick - 2 * number
            if 0 <= piece < 8:
                stage(number, piece)
        for number in behind.get(tick, ()):
            arrive(number)
        if tick == 8:
            mine = pl.ds(pl.multiple_of(zl * 256, 256), 256)
            filt_ref[...] = nt(fall[zl * 7, core, mine], perm[:, 0:256]) + nt(
                fall[1 - zl, core, mine], perm[:, 256:512]
            )

    for group in range(8):
        lines_of = slice(group * 32, group * 32 + 32)
        for half in range(2):
            block = sfin[(group // 2) * 2 + half, group % 2].reshape(32, 256)
            hi, lo = split(block)
            fin[0, lines_of, half * 256 : half * 256 + 256] = hi
            fin[1, lines_of, half * 256 : half * 256 + 256] = lo
    result = nt(fin[0], perm[...]) + nt(fin[1], perm[...])
    for group in range(8):
        lanes = slice(group * 512, group * 512 + 512)
        inter_ref[:, lanes] = result[group * 32 : group * 32 + 16]
        proj_ref[:, lanes] = result[group * 32 + 16 : group * 32 + 32]
    for copy in started:
        copy.wait_send()


def shards(
    orbital_block,
    cell_matrices,
    cell_nodes,
    shared_nodes,
    inv_sqrt_mass,
    potential,
    filter_center,
    filter_halfwidth,
):
    vm = pl.BlockSpec(memory_space=pltpu.VMEM)
    sm = pl.BlockSpec(memory_space=pltpu.SMEM)
    hbm = pl.BlockSpec(memory_space=pltpu.HBM)
    V = pltpu.VMEM
    dma = pltpu.SemaphoreType.DMA
    filtered, intersection, projected = pl.pallas_call(
        kernel,
        out_shape=(
            jax.ShapeDtypeStruct((256, 512), F32),
            jax.ShapeDtypeStruct((16, 4096), F32),
            jax.ShapeDtypeStruct((16, 4096), F32),
        ),
        in_specs=[hbm] * 6 + [sm, sm],
        out_specs=(vm, vm, vm),
        scratch_shapes=[
            V((256, 512), BF),
            V((125, 4, 125), BF),
            V((4, 125), jnp.int32),
            V((1, 64), jnp.int32),
            V((1, 256), F32),
            V((1, 256), F32),
            V((4, 128, 128), BF),
            V((8, 128), jnp.int32),
            V((8, 256), F32),
            V((2, 256, 256), BF),
            V((2, 256, 256), BF),
            V((2, 4, 128, 128), BF),
            V((2, 8, 128), jnp.int32),
            V((2, 8, 256), F32),
            V((512, 512), BF),
            V((512, 512), BF),
            V((512, 512), BF),
            V((384, 512), BF),
            V((384, 512), BF),
            V((512, 512), F32),
            V((384, 384), F32),
            V((512, 512), BF),
            V((512, 512), BF),
            V((2, 512, 128), BF),
            V((2, 64, 256), BF),
            V((64, 256), BF),
            V((256, 256), BF),
            V((64, 128), F32),
            V((128, 128), F32),
            V((512, 256), F32),
            V((512, 256), F32),
            V((512, 256), F32),
            V((512, 256), F32),
            V((512, 256), F32),
            V((512, 256), F32),
            V((512, 256), BF),
            V((FILTER_DEG + 1, 128, 256), BF),
            V((FILTER_DEG + 1, 128, 256), BF),
            V((8, 2, 512, 256), BF),
            V((512, 512), BF),
            V((8, 2, 4, 2, 64, 256), BF),
            V((8, 2, 2, 64, 256), BF),
            V((8, 2, 2, 2, 64, 256), BF),
            V((8, 2, 4, 2, 16, 256), BF),
            V((8, 2, 2, 16, 256), BF),
            V((8, 2, 2, 2, 16, 256), BF),
            V((8, 2, 2, 16, 256), F32),
            V((2, 256, 512), BF),
            dma((10,)),
            dma((5,)),
            dma((5,)),
            dma,
            dma,
            dma((FILTER_DEG + 1, 2)),
            dma((FILTER_DEG + 1, 2)),
            dma((2, 14)),
            dma((2, 14)),
            dma((8, 4)),
            dma((8, 4)),
            dma((8, 2, 2, 4)),
            dma((8, 2, 2, 4)),
        ],
        compiler_params=pltpu.CompilerParams(
            collective_id=0, has_side_effects=True, vmem_limit_bytes=28 * 1024 * 1024
        ),
    )(
        *(
            pltpu.with_memory_space_constraint(array, pltpu.HBM)
            for array in (
                orbital_block,
                jnp.transpose(cell_matrices, (1, 0, 2)),
                cell_nodes.T,
                shared_nodes,
                inv_sqrt_mass.reshape(1, 256),
                potential.reshape(1, 256),
            )
        ),
        filter_center,
        filter_halfwidth,
    )
    factor = 1.0 / 8192
    return filtered.astype(BF), intersection * factor, projected * factor


def solution(mesh):
    return jax.shard_map(
        shards,
        mesh=mesh,
        in_specs=(
            P("dom", "band"),
            P("dom", None, None),
            P(None, "dom"),
            P("dom", None),
            P("dom"),
            P("dom"),
            P(),
            P(),
        ),
        out_specs=(P("dom", "band"), P(("band", "dom"), None), P(("band", "dom"), None)),
        check_vma=False,
    )
```

```python
import jax
import jax.numpy as jnp
from jax import lax
from jax.experimental import pallas as pl
from jax.experimental.pallas import tpu as pltpu
from jax.sharding import PartitionSpec as P

FILTER_DEG = 4
BF = jnp.bfloat16
F32 = jnp.float32
MESH = pl.DeviceIdType.MESH
ORDER = (0, 7, 1, 6, 2, 5, 3, 4)


def nn(a, b):
    return lax.dot_general(a, b, (((1,), (0,)), ((), ())), preferred_element_type=F32)


def nt(a, b):
    return lax.dot_general(a, b, (((1,), (1,)), ((), ())), preferred_element_type=F32)


def split(a):
    hi = a.astype(BF)
    return hi, (a - hi.astype(F32)).astype(BF)


def rows_equal(count, row, base=0):
    index = lax.broadcasted_iota(jnp.int32, (count, row.shape[1]), 0) + base
    return jnp.where(index == row, 1.0, 0.0).astype(BF)


def kernel(
    x_hbm, m_hbm, nodes_hbm, shared_hbm, mass_hbm, pot_hbm, center_ref, half_ref,
    filt_ref, inter_ref, proj_ref,
    x_ref, m_ref, nodes_ref, shared_ref, mass_ref, pot_ref, mown, ints_own, vecs_own, xp, xc, m2, ints2, vecs2, perm,
    gt0, u0, gt1, u1, kmat, k1, ahi, alo, w2, wc, q0, eye, kgg_out, kgg_in, first_out,
    invb, invl, potb, potl, vcur, vprev, sbuf, gc_out, gc_in,
    fall, fat, p1, r1a, r1b, p2, r2a, r2b, sfin, fin,
    loc_sem, set_s, set_r, kgg_s, kgg_r, halo_s, halo_r,
    zs, zr, cs, cr, rs_s, rs_r,
):
    band = lax.axis_index("band")
    dom = lax.axis_index("dom")
    zh, core = band // 2, band % 2
    zl, x, y = dom % 2, (dom // 2) % 4, dom // 8
    z = zh * 2 + zl

    def device(zz, yy, xx, cc):
        return ((zz // 2) * 2 + cc, (yy * 4 + xx) * 2 + zz % 2)

    z_up, z_down = device((z + 1) % 8, y, x, core), device((z + 7) % 8, y, x, core)
    x_up, x_down = device(z, y, (x + 1) % 4, core), device(z, y, (x + 3) % 4, core)
    y_up, y_down = device(z, (y + 1) % 4, x, core), device(z, (y + 3) % 4, x, core)
    mate = device(z, y, x, 1 - core)
    pair = device(zh * 2 + 1 - zl, y, x, core)
    slab = y * 4 + x
    after, before = (slab + 1) % 16, (slab + 15) % 16
    nxt = device(z, after // 4, after % 4, core)
    prv = device(z, before // 4, before % 4, core)

    barrier = pltpu.get_barrier_semaphore()
    nxt_across = device(zh * 2 + 1 - zl, after // 4, after % 4, core)
    prv_across = device(zh * 2 + 1 - zl, before // 4, before % 4, core)
    friends = (
        z_up, z_down, x_up, x_down, y_up, y_down, mate, nxt, prv, nxt_across, prv_across,
    )
    for friend in friends:
        pl.semaphore_signal(barrier, inc=1, device_id=friend, device_id_type=MESH)

    def send(src, dst, ssem, rsem, to):
        copy = pltpu.make_async_remote_copy(
            src_ref=src, dst_ref=dst, send_sem=ssem, recv_sem=rsem,
            device_id=to, device_id_type=MESH,
        )
        copy.start()
        return copy

    started = []

    brought = [
        pltpu.make_async_copy(src, dst, loc_sem.at[4 + number])
        for number, (src, dst) in enumerate((
            (nodes_hbm, nodes_ref), (shared_hbm, shared_ref), (mass_hbm, mass_ref),
            (pot_hbm, pot_ref), (m_hbm, m_ref), (x_hbm, x_ref),
        ))
    ]
    for copy in brought:
        copy.start()
    ints_own[...] = jnp.full((8, 128), -1, jnp.int32)
    vecs_own[...] = jnp.zeros_like(vecs_own)
    mown[...] = jnp.zeros_like(mown)
    kgg_in[1, 64:128] = jnp.zeros((64, 128), F32)
    for copy in brought[0:4]:
        copy.wait()
    ints_own[0:4, 0:125] = nodes_ref[...]
    ints_own[4:5, 0:64] = shared_ref[...]
    ints_own[5:6, 64:128] = shared_ref[...]
    vecs_own[0:1] = mass_ref[...]
    vecs_own[1:2] = pot_ref[...]
    brought[4].wait()
    for c in range(4):
        mown[c, 0:125, 0:125] = m_ref[:, c, :]
    cells = pl.ds(core * 2, 2)
    pl.semaphore_wait(barrier, len(friends))
    setup = [
        send(ints_own, ints2.at[zl], set_s.at[0], set_r.at[0], pair),
        send(vecs_own, vecs2.at[zl], set_s.at[1], set_r.at[1], pair),
        send(mown.at[cells], m2.at[zl, cells], set_s.at[2], set_r.at[2], pair),
    ]
    own = [
        pltpu.make_async_copy(ints_own, ints2.at[zl], loc_sem.at[0]),
        pltpu.make_async_copy(vecs_own, vecs2.at[zl], loc_sem.at[1]),
        pltpu.make_async_copy(mown, m2.at[zl], loc_sem.at[2]),
    ]
    for copy in own:
        copy.start()
    brought[5].wait()
    col = lax.broadcasted_iota(jnp.int32, (512, 512), 0)
    place = lax.broadcasted_iota(jnp.int32, (512, 512), 1)
    goal = ((col >> 4) & 1) * 256 + (col >> 5) * 16 + (col & 15)
    perm[...] = jnp.where(goal == place, 1.0, 0.0).astype(BF)
    for half in range(2):
        xp[half] = nn(x_ref[...], perm[:, half * 256 : half * 256 + 256]).astype(BF)
    setup.append(send(xp.at[1 - zl], xc.at[zl], set_s.at[3], set_r.at[3], pair))
    own.append(pltpu.make_async_copy(xp.at[zl], xc.at[zl], loc_sem.at[3]))
    own[3].start()
    started += setup
    for c in range(4):
        lanes = slice(c * 128, c * 128 + 128)
        hot = rows_equal(384, ints_own[c : c + 1, :])
        gt1[:, lanes] = hot
        u1[256:384, lanes] = nn(hot[256:384], mown[c]).astype(BF)
    edge = nt(u1[256:384, :], gt1[...])
    kgg_out[...] = edge[0:64, 256:384]
    edge_hi, edge_lo = split(edge[0:64, 0:256])
    unit = lax.broadcasted_iota(jnp.int32, (256, 256), 0)
    eye[...] = jnp.where(unit == lax.broadcasted_iota(jnp.int32, (256, 256), 1), 1.0, 0.0).astype(BF)
    pick = nt(eye[0:128, 0:128], rows_equal(256, ints_own[4:5, :]))[0:64].astype(BF)
    mass_own = jnp.broadcast_to(jnp.transpose(vecs_own[...])[:, 0:1], (256, 256))
    for half in range(2):
        scaled = (mass_own * xp[half].astype(F32)).astype(BF)
        first_out[0, half] = nn(pick, scaled).astype(BF)
        first_out[1, half] = (nn(edge_hi, scaled) + nn(edge_lo, scaled)).astype(BF)
    outer = zl * after + (1 - zl) * before
    landing = pl.ds(pl.multiple_of(zl * 64, 64), 64)
    kggs = []
    copies = []
    for half in range(2):
        to = device(zh * 2 + half, outer // 4, outer % 4, core)
        kggs.append(send(
            kgg_out, kgg_in.at[zl, 0:64], kgg_s.at[half], kgg_r.at[zl], to
        ))
        copies.append(send(
            first_out.at[zl, half], gc_in.at[0, landing],
            halo_s.at[0, half], halo_r.at[0, zl], to,
        ))
    started += kggs + copies
    for copy in own[0:2]:
        copy.wait()
    for copy in setup[0:2]:
        copy.wait_recv()

    q1t = rows_equal(256, ints2[1, 4:5, :])
    q0t = rows_equal(256, ints2[0, 4:5, :])
    q0t_right = rows_equal(256, ints2[0, 5:6, :])
    for c in range(4):
        lanes = slice(c * 128, c * 128 + 128)
        row = ints2[0, c : c + 1, :]
        top = rows_equal(256, row)
        ghost = rows_equal(128, row, 256)
        bottom = nn(q1t, ghost).astype(BF)
        gt0[0:256, lanes] = top
        gt0[256:512, lanes] = bottom
        gt1[:, lanes] = rows_equal(384, ints2[1, c : c + 1, :])
    setup[2].wait_recv()
    half_cells = m2.at[1 - zl, cells]
    shared_cells = send(half_cells, half_cells, set_s.at[4], set_r.at[4], mate)
    started.append(shared_cells)
    own[2].wait()
    shared_cells.wait_recv()
    for c in range(4):
        lanes = slice(c * 128, c * 128 + 128)
        u1[:, lanes] = nn(gt1[:, lanes], m2[1, c]).astype(BF)
    for c in range(4):
        lanes = slice(c * 128, c * 128 + 128)
        u0[:, lanes] = nn(gt0[:, lanes], m2[0, c]).astype(BF)
    k1[...] = nt(u1[...], gt1[...])
    kmat[...] = nt(u0[...], gt0[...])
    kmat[256:512, 256:512] += k1[0:256, 0:256]
    w2[0, 0:256] = q0t_right
    hi, lo = split(k1[0:256, 256:384])
    w2[0, 256:512] = hi
    w2[1, 256:512] = lo
    q0[...] = nt(eye[0:128, 0:128], q0t_right)[64:128].astype(BF)
    hi, lo = split(k1[256:320, 0:256])
    wc[0] = hi
    wc[1] = lo

    center, halfwidth = center_ref[0], half_ref[0]
    own[3].wait()
    setup[3].wait_recv()
    for slot in range(2):
        nodes = slice(slot * 256, slot * 256 + 256)
        columns = jnp.transpose(vecs2[slot])
        mass = jnp.broadcast_to(columns[:, 0:1], (256, 256))
        pot = jnp.broadcast_to(columns[:, 1:2], (256, 256))
        invb[nodes] = mass
        potb[nodes] = pot
        invl[nodes] = mass / halfwidth
        potl[nodes] = (pot - center) / halfwidth
        start = xc[slot].astype(F32)
        vcur[nodes] = start
        sbuf[nodes] = (mass * start).astype(BF)

    def push(step, half):
        if half == 1:
            out = nn(wc[0], sbuf[256:512]) + nn(wc[1], sbuf[256:512])
            rows, landing, to = slice(0, 64), slice(64, 128), nxt
        else:
            out = nn(q0[...], sbuf[0:256])
            rows, landing, to = slice(64, 128), slice(0, 64), prv
        gc_out[step, rows] = out.astype(BF)
        copy = send(
            gc_out.at[step, rows], gc_in.at[step, landing],
            halo_s.at[step, half], halo_r.at[step, half], to,
        )
        started.append(copy)
        return copy

    def inside():
        return nn(ahi[...], sbuf[...]) + nn(alo[...], sbuf[...])

    def whole(inner, half, came):
        nodes = slice(half * 256, half * 256 + 256)
        total = inner[nodes] + nn(w2[0, nodes], came)
        if half == 1:
            total = total + nn(w2[1, nodes], came)
        return nodes, total

    def expected(src, dst, rsem):
        return pltpu.make_async_remote_copy(
            src_ref=src, dst_ref=dst, send_sem=halo_s.at[0, 0], recv_sem=rsem,
            device_id=nxt, device_id_type=MESH,
        )

    for side in range(2):
        expected(kgg_out, kgg_in.at[side, 0:64], kgg_r.at[side]).wait_recv()
    copies = [
        expected(first_out.at[0, 0], gc_in.at[0, side * 64 : side * 64 + 64], halo_r.at[0, side])
        for side in range(2)
    ]
    hi, lo = split(kgg_in[1])
    hi, lo = split(nn(q0t, hi) + nn(q0t, lo))
    kmat[0:256, 0:256] += nt(hi, q0t) + nt(lo, q0t)
    hi, lo = split(kmat[...])
    ahi[...] = hi
    alo[...] = lo

    for step in range(FILTER_DEG):
        inner = inside()
        for copy in copies:
            copy.wait_recv()
        came = gc_in[step]
        copies = []
        for half in (1, 0):
            nodes, total = whole(inner, half, came)
            image = invl[nodes] * total + potl[nodes] * vcur[nodes]
            if step > 0:
                image = 2.0 * image - vprev[nodes]
            if step < FILTER_DEG - 1:
                vprev[nodes] = vcur[nodes]
            else:
                filtered = image.astype(BF)
                fall[0, core, nodes] = filtered
                image = filtered.astype(F32)
            vcur[nodes] = image
            sbuf[nodes] = (invb[nodes] * image).astype(BF)
            copies.append(push(step + 1, half))

    tours = ([], [])

    def onward(way, slot, half):
        landing = (slot + 7) % 8 if way == 0 else (slot + 1) % 8
        nodes = slice(half * 128, half * 128 + 128)
        number = len(tours[way])
        copy = send(
            fall.at[slot, core, nodes], fall.at[landing, core, nodes],
            zs.at[way, number], zr.at[way, number], (z_up, z_down)[way],
        )
        tours[way].append((copy, landing, half))
        started.append(copy)

    others = {}

    def across(slot, half):
        block = fall.at[slot, core, half * 128 : half * 128 + 128]
        others[slot, half] = send(block, block, cs.at[slot, half], cr.at[slot, half], mate)
        started.append(others[slot, half])

    def arrive(number):
        for way in range(2):
            copy, slot, half = tours[way][number]
            copy.wait_recv()
            if number < 10:
                onward(way, slot, half)
            across(slot, half)

    for half in range(4):
        onward(0, 0, half)
        onward(1, 0, 3 - half)
        across(0, half)

    lines = (((x, x_up, x_down), (y, y_up, y_down)), ((y, y_up, y_down), (x, x_up, x_down)))
    flights = {}

    def ring_first(piece, mat, level):
        pos, right, left = lines[mat ^ (piece & 1)][level]
        part, in_a = (p1, r1a) if level == 0 else (p2, r2a)
        far = (pos + 2) % 4
        sem = (piece, mat, level)
        pairs = []
        for side, to in ((0, right), (1, left)):
            pairs.append(send(
                part.at[piece, mat, far, side], in_a.at[piece, mat, side],
                rs_s.at[(*sem, side)], rs_r.at[(*sem, side)], to,
            ))
        flights[(*sem, 0)] = pairs
        started.extend(pairs)

    def ring_second(piece, mat, level):
        pos, right, left = lines[mat ^ (piece & 1)][level]
        part, in_a, in_b = (p1, r1a, r1b) if level == 0 else (p2, r2a, r2b)
        sem = (piece, mat, level)
        pairs = []
        for side, to in ((0, right), (1, left)):
            near = (pos + 1) % 4 if side == 0 else (pos + 3) % 4
            flights[(*sem, 0)][side].wait_recv()
            whole = part[piece, mat, near, side].astype(F32) + in_a[piece, mat, side].astype(F32)
            part[piece, mat, near, side] = whole.astype(BF)
            pairs.append(send(
                part.at[piece, mat, near], in_b.at[piece, mat, side],
                rs_s.at[(*sem, 2 + side)], rs_r.at[(*sem, 2 + side)], to,
            ))
        flights[(*sem, 1)] = pairs
        started.extend(pairs)

    def ring_last(piece, mat, level):
        pos, right, left = lines[mat ^ (piece & 1)][level]
        part, in_b = (p1, r1b) if level == 0 else (p2, r2b)
        for copy in flights[(piece, mat, level, 1)]:
            copy.wait_recv()
        return (
            part[piece, mat, pos].astype(F32)
            + in_b[piece, mat, 0].astype(F32)
            + in_b[piece, mat, 1].astype(F32)
        )

    def place(product, piece, mat, side):
        for yy in range(4):
            k = yy * 64
            if mat ^ (piece & 1):
                p1[piece, mat, yy, side] = product[k : k + 64]
            else:
                for xx in range(4):
                    rows = product[k + xx * 16 : k + xx * 16 + 16]
                    p1[piece, mat, xx, side, yy * 16 : yy * 16 + 16] = rows

    def landed(slot):
        for part in range(4):
            others[slot, part].wait_recv()

    def stage(number, piece):
        slot = ORDER[piece]
        if number == 0:
            for turn in range(2):
                side = core if turn == 0 else 1 - core
                if turn == 1:
                    landed(slot)
                product = nn(fat[...], fall[slot, side]).astype(BF)
                for mat in range(2):
                    place(product[mat * 256 : mat * 256 + 256], piece, mat, side)
            for mat in range(2):
                ring_first(piece, mat, 0)
        elif number == 1:
            for mat in range(2):
                ring_second(piece, mat, 0)
        elif number == 2:
            for mat in range(2):
                level_sum = ring_last(piece, mat, 0).astype(BF)
                for to in range(4):
                    p2[piece, mat, to] = level_sum[:, to * 16 : to * 16 + 16]
                ring_first(piece, mat, 1)
        elif number == 3:
            for mat in range(2):
                ring_second(piece, mat, 1)
        else:
            source = (z + slot) % 8
            for mat in range(2):
                sfin[source, :, mat] = ring_last(piece, mat, 1)

    inner = inside()
    fat[0:256] = nt(eye[...], fall[0, core]).astype(BF)
    place(nn(fat[0:256], fall[0, core]).astype(BF), 0, 0, core)
    landed(0)
    place(nn(fat[0:256], fall[0, 1 - core]).astype(BF), 0, 0, 1 - core)
    ring_first(0, 0, 0)
    arrive(0)
    for copy in copies:
        copy.wait_recv()
    came = gc_in[FILTER_DEG]
    for half in (1, 0):
        nodes, total = whole(inner, half, came)
        sbuf[nodes] = (invb[nodes] * total + potb[nodes] * vcur[nodes]).astype(BF)
    arrive(1)
    fat[256:512] = nt(eye[...], sbuf[...]).astype(BF)
    for side in range(2):
        place(nn(fat[256:512], fall[0, side]).astype(BF), 0, 1, side)
    ring_first(0, 1, 0)
    arrive(2)

    ahead = {1: (3,), 3: (7,), 5: (11,)}
    behind = {1: (4,), 2: (5, 6), 3: (8,), 4: (9, 10), 5: (12,), 6: (13,)}
    for tick in range(1, 16):
        for number in ahead.get(tick, ()):
            arrive(number)
        for number in range(4, -1, -1):
            piece = tick - 2 * number
            if 0 <= piece < 8:
                stage(number, piece)
        for number in behind.get(tick, ()):
            arrive(number)
        if tick == 8:
            mine = pl.ds(pl.multiple_of(zl * 256, 256), 256)
            filt_ref[...] = nt(fall[zl * 7, core, mine], perm[:, 0:256]) + nt(
                fall[1 - zl, core, mine], perm[:, 256:512]
            )

    for group in range(8):
        lines_of = slice(group * 32, group * 32 + 32)
        for half in range(2):
            block = sfin[(group // 2) * 2 + half, group % 2].reshape(32, 256)
            hi, lo = split(block)
            fin[0, lines_of, half * 256 : half * 256 + 256] = hi
            fin[1, lines_of, half * 256 : half * 256 + 256] = lo
    result = nt(fin[0], perm[...]) + nt(fin[1], perm[...])
    for group in range(8):
        lanes = slice(group * 512, group * 512 + 512)
        inter_ref[:, lanes] = result[group * 32 : group * 32 + 16]
        proj_ref[:, lanes] = result[group * 32 + 16 : group * 32 + 32]
    for copy in started:
        copy.wait_send()


def shards(
    orbital_block,
    cell_matrices,
    cell_nodes,
    shared_nodes,
    inv_sqrt_mass,
    potential,
    filter_center,
    filter_halfwidth,
):
    vm = pl.BlockSpec(memory_space=pltpu.VMEM)
    sm = pl.BlockSpec(memory_space=pltpu.SMEM)
    hbm = pl.BlockSpec(memory_space=pltpu.HBM)
    V = pltpu.VMEM
    dma = pltpu.SemaphoreType.DMA
    filtered, intersection, projected = pl.pallas_call(
        kernel,
        out_shape=(
            jax.ShapeDtypeStruct((256, 512), F32),
            jax.ShapeDtypeStruct((16, 4096), F32),
            jax.ShapeDtypeStruct((16, 4096), F32),
        ),
        in_specs=[hbm] * 6 + [sm, sm],
        out_specs=(vm, vm, vm),
        scratch_shapes=[
            V((256, 512), BF),
            V((125, 4, 125), BF),
            V((4, 125), jnp.int32),
            V((1, 64), jnp.int32),
            V((1, 256), F32),
            V((1, 256), F32),
            V((4, 128, 128), BF),
            V((8, 128), jnp.int32),
            V((8, 256), F32),
            V((2, 256, 256), BF),
            V((2, 256, 256), BF),
            V((2, 4, 128, 128), BF),
            V((2, 8, 128), jnp.int32),
            V((2, 8, 256), F32),
            V((512, 512), BF),
            V((512, 512), BF),
            V((512, 512), BF),
            V((384, 512), BF),
            V((384, 512), BF),
            V((512, 512), F32),
            V((384, 384), F32),
            V((512, 512), BF),
            V((512, 512), BF),
            V((2, 512, 128), BF),
            V((2, 64, 256), BF),
            V((64, 256), BF),
            V((256, 256), BF),
            V((64, 128), F32),
            V((2, 128, 128), F32),
            V((2, 2, 64, 256), BF),
            V((512, 256), F32),
            V((512, 256), F32),
            V((512, 256), F32),
            V((512, 256), F32),
            V((512, 256), F32),
            V((512, 256), F32),
            V((512, 256), BF),
            V((FILTER_DEG + 1, 128, 256), BF),
            V((FILTER_DEG + 1, 128, 256), BF),
            V((8, 2, 512, 256), BF),
            V((512, 512), BF),
            V((8, 2, 4, 2, 64, 256), BF),
            V((8, 2, 2, 64, 256), BF),
            V((8, 2, 2, 2, 64, 256), BF),
            V((8, 2, 4, 2, 16, 256), BF),
            V((8, 2, 2, 16, 256), BF),
            V((8, 2, 2, 2, 16, 256), BF),
            V((8, 2, 2, 16, 256), F32),
            V((2, 256, 512), BF),
            dma((10,)),
            dma((5,)),
            dma((5,)),
            dma((2,)),
            dma((2,)),
            dma((FILTER_DEG + 1, 2)),
            dma((FILTER_DEG + 1, 2)),
            dma((2, 14)),
            dma((2, 14)),
            dma((8, 4)),
            dma((8, 4)),
            dma((8, 2, 2, 4)),
            dma((8, 2, 2, 4)),
        ],
        compiler_params=pltpu.CompilerParams(
            collective_id=0, has_side_effects=True, vmem_limit_bytes=28 * 1024 * 1024
        ),
    )(
        *(
            pltpu.with_memory_space_constraint(array, pltpu.HBM)
            for array in (
                orbital_block,
                jnp.transpose(cell_matrices, (1, 0, 2)),
                cell_nodes.T,
                shared_nodes,
                inv_sqrt_mass.reshape(1, 256),
                potential.reshape(1, 256),
            )
        ),
        filter_center,
        filter_halfwidth,
    )
    factor = 1.0 / 8192
    return filtered.astype(BF), intersection * factor, projected * factor


def solution(mesh):
    return jax.shard_map(
        shards,
        mesh=mesh,
        in_specs=(
            P("dom", "band"),
            P("dom", None, None),
            P(None, "dom"),
            P("dom", None),
            P("dom"),
            P("dom"),
            P(),
            P(),
        ),
        out_specs=(P("dom", "band"), P(("band", "dom"), None), P(("band", "dom"), None)),
        check_vma=False,
    )
```
